128 devices in a mesh: sub: 16 (over y, z), grp: 8 (over x, core).
Axes of the slice: x: 4, y: 4, z: 4, core: 2. Of those that a mesh axis runs over, the one named last changes fastest.
Arguments:
- interior_res: bfloat16 [1024, 32, 256], P(('sub', 'grp')), may hold values from -6 to 6
- interface_res: bfloat16 [1024, 32, 512], P(('sub', 'grp')), may hold values from -6 to 6
- interior_inv: bfloat16 [1024, 256, 256], P(('sub', 'grp')), may hold values from -0.375 to 0.375
- coupling: bfloat16 [1024, 512, 256], P(('sub', 'grp')), may hold values from -0.375 to 0.375
- schur_inv: bfloat16 [1024, 512, 512], P(('sub', 'grp')), may hold values from -0.25 to 0.25
- coarse_inv: bfloat16 [512, 128, 128], P('grp'), may hold values from -0.5 to 0.5
- coarse_part: int32 [524288, 1], P(('sub', 'grp')), may hold values from 0 to 127; in each aligned block of 4096 rows (0 to 4095, 4096 to 8191, ...) at most 64 rows name the same one
- coarse_slot: int32 [524288], P(('sub', 'grp')), may hold values from 0 to 511
- live_count: int32 [1024], P(('sub', 'grp')), may hold values from 128 to 512
Outputs:
- interior_update: bfloat16 [1024, 32, 256], P(('sub', 'grp'))
- interface_update: bfloat16 [1024, 32, 512], P(('sub', 'grp'))
The draws below stay inside these ranges and needn't reach their ends.
Inputs may be any that keep to these rules, and one draw needn't show every extreme that they name: `coarse_part`: in each device's aligned block of 4096 rows no section is named by more than 64 rows, a bound that some block reaches.
All inputs are finite; a program needn't handle non-finite values.
Results may differ from the reference program's by a relative error of at most 0.0076.
Values may be sent and summed in bfloat16 or wider, within the bound.
No kernel may reach another device: no remote copies, remote signals or barrier semaphores. Data moves between devices by JAX's collectives and lax.ppermute only.
A program may use at most 64 MiB of HBM per device.

```python
import math
import jax
import jax.numpy as jnp
import numpy as np
from jax import lax

K = 32
NI = 256
NB = 512
CB = 128
SUB_DEV = 8
SUBS = 1024
ROWS_DEV = 4096
ROWS = 524288
NPART = 128
CAP = 64
NC = 65536
NCO = 8192
NCP = 512
NCBLK = 512
N_GRP = 8


def place_ends(result, own_key, smallest, high):
    longest = result.shape.index(max(result.shape))
    spots = []
    for shift in (0, 1):
        where = [jax.random.randint(jax.random.fold_in(own_key, axis), (), 0, length) for axis, length in enumerate(result.shape)]
        where[longest] = (where[longest] + shift) % result.shape[longest]
        spots.append(tuple(where))
    return result.at[spots[0]].set(smallest).at[spots[1]].set(high)


def block_levels(own_key, dims, shards, smallest, high):
    def one(position, parts):
        heights = jax.random.uniform(jax.random.fold_in(jax.random.fold_in(own_key, 6), position), (parts,), jnp.float32, smallest / len(shards), high / len(shards))
        return jnp.repeat(jnp.exp(heights), dims[position] // parts).reshape((-1,) + (1,) * (len(dims) - position - 1))

    loudness = one(*shards[0])
    for cut in shards[1:]:
        loudness = loudness * one(*cut)
    return loudness


def shared_out(stream_key, own, number, rows, amount, top, most, skew):
    order = jax.random.permutation(stream_key, amount)
    crowded, ordinary = load_shares(amount, rows * top, most, skew, True), load_shares(amount, rows * top, most, skew, False)
    places = jnp.arange(amount)

    def named(tallies, turn):
        used = int((tallies > 0).sum())
        fixed = max(1, used // 4)
        shifted = fixed + (places - fixed + turn * (used - fixed)) % max(1, amount - fixed)
        return jnp.zeros((amount,), jnp.int32).at[order[jnp.where(places < fixed, places, shifted)]].set(jnp.asarray(tallies, jnp.int32))

    tallies = jnp.where(number % 4 == 0, named(crowded, number // 4), named(ordinary, number - number // 4 - 1))
    mixed = jax.random.permutation(jax.random.fold_in(own, 3), amount)
    source_of, receiver = mixed[0:amount // 2 * 2:2], mixed[1:amount // 2 * 2:2]
    margin = jnp.minimum(tallies[source_of] - 1, most - tallies[receiver]) // 2
    margin = jnp.where((source_of == order[0]) | (receiver == order[0]) | (tallies[receiver] == 0), 0, jnp.maximum(margin, 0))
    shifted = jax.random.randint(jax.random.fold_in(own, 4), (amount // 2,), 0, 1 << 20) % (margin + 1)
    tallies = tallies.at[source_of].add(-shifted).at[receiver].add(shifted)
    items = jnp.searchsorted(jnp.cumsum(tallies), jnp.arange(rows * top), side="right").astype(jnp.int32)
    grid = items.reshape(top, rows).T
    grid = grid[jax.random.permutation(jax.random.fold_in(own, 1), rows)]
    turn = jax.random.randint(jax.random.fold_in(own, 2), (rows, 1), 0, top)
    return jnp.take_along_axis(grid, (jnp.arange(top)[None, :] + turn) % top, axis=1)


def load_shares(number_of, total, most, lean, full):
    portions = [(1 << 20) // math.isqrt(standing ** lean) + 1 for standing in range(1, number_of + 1)]
    largest = most if full else min(most, max(-(-total // number_of), total * portions[0] // sum(portions)))
    least = 1 if total - largest >= number_of - 1 else 0
    given, rest = [largest] + [least] * (number_of - 1), total - largest - least * (number_of - 1)
    while rest > 0:
        free = [i for i in range(1, number_of) if given[i] < largest] or [i for i in range(1, number_of) if given[i] < most]
        mass, left = sum([portions[i] for i in free]), rest
        for i in free:
            extra = min(most - given[i], max(1, left * portions[i] // mass), rest)
            given[i] = given[i] + extra
            rest = rest - extra
    return np.array(given)


def noise(key, dims, deviation, bound, split=(), kind=jnp.bfloat16):
    level = block_levels(key, dims, split, -0.22, 0.18) if split else 1.0
    result = jax.random.normal(key, dims, jnp.float32) * deviation * level
    return jnp.minimum(jnp.maximum(result, -bound), bound).astype(kind)


def setup_inputs(seed: int = 0) -> dict:
    splits = jax.random.split(jax.random.key(seed), 10)
    interior_res = noise(splits[0], (SUBS, K, NI), 1.0, 6.0, ((0, 128),))
    interface_res = noise(splits[1], (SUBS, K, NB), 1.0, 6.0, ((0, 128),))
    interior_inv = noise(splits[2], (SUBS, NI, NI), NI ** -0.5, 0.375, ((0, 128),))
    coupling = noise(splits[3], (SUBS, NB, NI), NI ** -0.5, 0.375, ((0, 128),))
    schur_inv = noise(splits[4], (SUBS, NB, NB), NB ** -0.5, 0.25, ((0, 128),))
    coarse_inv = noise(splits[5], (NCBLK, CB, CB), CB ** -0.5, 0.5, ((0, 8),))
    coarse_part_keys = jax.random.split(jax.random.fold_in(splits[6], 1), ROWS // ROWS_DEV)
    coarse_part_turns = jax.random.permutation(jax.random.fold_in(splits[6], 3), ROWS // ROWS_DEV)
    coarse_part = jax.vmap(lambda own, number: shared_out(jax.random.fold_in(splits[6], 2), own, number, ROWS_DEV, NPART, 1, CAP, 2))(coarse_part_keys, coarse_part_turns).reshape((ROWS, 1))
    coarse_slot = place_ends(jax.random.randint(splits[7], (ROWS,), 0, NCP), jax.random.fold_in(splits[7], 1), 0, NCP - 1).astype(jnp.int32)
    live_count = place_ends(jax.random.randint(splits[8], (SUBS,), NB // 4, NB + 1), jax.random.fold_in(splits[8], 1), NB // 4, NB).astype(jnp.int32)
    return dict(interior_res=interior_res, interface_res=interface_res, interior_inv=interior_inv, coupling=coupling, schur_inv=schur_inv, coarse_inv=coarse_inv, coarse_part=coarse_part, coarse_slot=coarse_slot, live_count=live_count)


def front_part(pieces):
    inverse, joined, inner_res, face_res, counts = pieces
    interior_pre = jnp.einsum("sij,skj->ski", inverse.astype(jnp.float32), inner_res.astype(jnp.float32)).astype(jnp.bfloat16)
    condensed = face_res.astype(jnp.float32) - jnp.einsum("sbi,ski->skb", joined.astype(jnp.float32), interior_pre.astype(jnp.float32))
    alive_mask = jnp.arange(NB, dtype=jnp.int32)[None, None, :] < counts[:, None, None]
    return jnp.where(alive_mask, condensed, 0.0).astype(jnp.bfloat16)


def back_part(pieces):
    inverse, joined, schur_part, inner_res, condensed, correction, counts = pieces
    alive_mask = jnp.arange(NB, dtype=jnp.int32)[None, None, :] < counts[:, None, None]
    local_term = jnp.einsum("sbc,skc->skb", schur_part.astype(jnp.float32), condensed.astype(jnp.float32))
    interface_update = jnp.where(alive_mask, local_term + correction.astype(jnp.float32), 0.0).astype(jnp.bfloat16)
    extended = inner_res.astype(jnp.float32) - jnp.einsum("sbi,skb->ski", joined.astype(jnp.float32), interface_update.astype(jnp.float32))
    extended = extended.astype(jnp.bfloat16)
    interior_update = jnp.einsum("sij,skj->ski", inverse.astype(jnp.float32), extended.astype(jnp.float32)).astype(jnp.bfloat16)
    return interior_update, interface_update


def grouped(array):
    return array.reshape((SUBS // SUB_DEV, SUB_DEV) + array.shape[1:])


def reference(interior_res, interface_res, interior_inv, coupling, schur_inv, coarse_inv, coarse_part, coarse_slot, live_count):
    condensed = lax.map(front_part, (grouped(interior_inv), grouped(coupling), grouped(interior_res), grouped(interface_res), grouped(live_count)))
    condensed = condensed.reshape(SUBS, K, NB)
    flat_rows = jnp.transpose(condensed, (0, 2, 1)).reshape(ROWS, K).astype(jnp.float32)
    section = coarse_part[:, 0].astype(jnp.int32)
    coarse_index = ((section % N_GRP) * NCO + (section // N_GRP) * NCP + coarse_slot).astype(jnp.int32)
    coarse_sum = jax.ops.segment_sum(flat_rows, coarse_index, num_segments=NC)
    coarse_rhs = coarse_sum.astype(jnp.bfloat16)
    coarse_sol = jnp.einsum("bij,bjk->bik", coarse_inv.astype(jnp.float32), coarse_rhs.reshape(NCBLK, CB, K).astype(jnp.float32))
    coarse_sol = coarse_sol.reshape(NC, K).astype(jnp.bfloat16)
    correction = jnp.transpose(coarse_sol[coarse_index].reshape(SUBS, NB, K), (0, 2, 1))
    interior_update, interface_update = lax.map(back_part, (grouped(interior_inv), grouped(coupling), grouped(schur_inv), grouped(interior_res), grouped(condensed), grouped(correction), grouped(live_count)))
    return interior_update.reshape(SUBS, K, NI), interface_update.reshape(SUBS, K, NB)
```

```python
import jax
import jax.numpy as jnp
from jax import lax
from jax.experimental import pallas as pl
from jax.experimental.pallas import tpu as pltpu
from jax.sharding import PartitionSpec as P

F32 = jnp.float32
BF16 = jnp.bfloat16
AXES = ("sub", "grp")
CAP = 64
VMEM = pltpu.VMEM
HALF = 64


def dot_nn(left, right):
    return lax.dot_general(left, right, (((1,), (0,)), ((), ())), preferred_element_type=F32)


def dot_nt(left, right):
    return lax.dot_general(left, right, (((1,), (1,)), ((), ())), preferred_element_type=F32)


def low_half(rows):
    return lax.broadcasted_iota(jnp.int32, (rows, 128), 1) < HALF


def swap_pair(first, second):
    mask = low_half(first.shape[0])
    even = jnp.where(mask, first, pltpu.roll(second, HALF, 1))
    odd = jnp.where(mask, pltpu.roll(first, HALF, 1), second)
    return even, odd


def one_hot(count, index):
    rows = lax.broadcasted_iota(jnp.int32, (count, index.shape[1]), 0).astype(BF16)
    return jnp.where(rows == index.astype(BF16), 1.0, 0.0).astype(BF16)


def front_kernel(
    live_ref, part_ref, slot_ref, ires_ref, fres_ref, inv_hbm, cpl_hbm,
    cond_ref, out_ref, dest_ref,
    inv_ref, cpl_ref, lhs_ref, acc_ref, sem,
):
    subs, vecs, inner = ires_ref.shape
    face = fres_ref.shape[2]
    loads = []
    for s in range(subs):
        one = pltpu.make_async_copy(inv_hbm.at[s], inv_ref.at[s], sem.at[0, s])
        two = pltpu.make_async_copy(cpl_hbm.at[s], cpl_ref.at[s], sem.at[1, s])
        one.start()
        two.start()
        loads.append((one, two))

    width = 256
    sections = out_ref.shape[0]
    upper = (
        lax.broadcasted_iota(jnp.int32, (width, width), 0)
        <= lax.broadcasted_iota(jnp.int32, (width, width), 1)
    ).astype(F32).astype(BF16)
    ones = jnp.ones((width, width), BF16)
    section_row = lax.broadcasted_iota(jnp.int32, (sections, width), 0)
    before = jnp.zeros((sections, width), F32)
    for c in range(subs * face // width):
        cols = pl.ds(c * width, width)
        section = part_ref[:, cols]
        hot = section_row == section
        hot16 = jnp.where(hot, 1.0, 0.0).astype(BF16)
        counted = dot_nn(hot16, upper) + before
        place = jnp.sum(jnp.where(hot, counted, 0.0), axis=0, keepdims=True) - 1.0
        before = before + dot_nn(hot16, ones)
        dest_ref[:, cols] = section * CAP + place.astype(jnp.int32)

    groups = sections // 4
    group_row = lax.broadcasted_iota(jnp.int32, (groups, face), 0)
    for s in range(subs):
        loads[s][0].wait()
        loads[s][1].wait()
        pre = dot_nt(ires_ref[s], inv_ref[s]).astype(BF16)
        cond = fres_ref[s].astype(F32) - dot_nt(pre, cpl_ref[s])
        alive = lax.broadcasted_iota(jnp.int32, (vecs, face), 1) < live_ref[s]
        cond = jnp.where(alive, cond, 0.0).astype(BF16)
        cond_ref[s] = cond
        cols = pl.ds(s * face, face)
        dest = dest_ref[:, cols]
        group = lax.shift_right_logical(dest, 8)
        hot = one_hot(256, jnp.bitwise_and(dest, 255))
        group16 = jnp.broadcast_to(group.astype(BF16), (vecs, face))
        for a in range(groups):
            lhs_ref[pl.ds(a * vecs, vecs), :] = jnp.where(group16 == a, cond, jnp.zeros_like(cond))
        slot = slot_ref[:, cols]
        mine = group_row == group
        high = jnp.where(mine, lax.shift_right_logical(slot, 8).astype(F32), 0.0).astype(BF16)
        low = jnp.where(mine, jnp.bitwise_and(slot, 255).astype(F32), 0.0).astype(BF16)
        lhs_ref[pl.ds(groups * vecs, groups), :] = high
        lhs_ref[pl.ds(groups * vecs + groups, groups), :] = low
        part = dot_nt(lhs_ref[...], hot)
        if s == 0:
            acc_ref[...] = part
        else:
            acc_ref[...] += part

    kh = vecs // 2
    base = groups * vecs
    for a in range(groups):
        for h in range(2):
            lanes = pl.ds(h * 128, 128)
            first = acc_ref[pl.ds(a * vecs, kh), lanes]
            second = acc_ref[pl.ds(a * vecs + kh, kh), lanes]
            even, odd = swap_pair(first, second)
            slot_even, slot_odd = swap_pair(
                jnp.broadcast_to(acc_ref[pl.ds(base + a, 1), lanes], (8, 128)),
                jnp.broadcast_to(acc_ref[pl.ds(base + groups + a, 1), lanes], (8, 128)),
            )
            p = 4 * a + 2 * h
            out_ref[p, 0:kh, :] = even.astype(BF16)
            out_ref[p, kh:kh + 8, :] = slot_even.astype(BF16)
            out_ref[p + 1, 0:kh, :] = odd.astype(BF16)
            out_ref[p + 1, kh:kh + 8, :] = slot_odd.astype(BF16)


def local_kernel(schur_ref, cond_ref, out_ref):
    out_ref[0] = dot_nt(cond_ref[0], schur_ref[0])


def middle_kernel(recv_ref, inv_ref, out_ref, lhs_ref, hot_ref, high_ref):
    senders = recv_ref.shape[0]
    kh = out_ref.shape[1]
    vecs = 2 * kh
    for j in range(senders // 2):
        cols = pl.ds(j * 128, 128)
        first = recv_ref[2 * j].astype(F32)
        second = recv_ref[2 * j + 1].astype(F32)
        even, odd = swap_pair(first, second)
        high = even[kh:kh + 1]
        hot_ref[:, cols] = one_hot(256, odd[kh:kh + 1])
        high_ref[:, cols] = jnp.broadcast_to(high, (8, 128))
        data = jnp.concatenate([even[:kh], odd[:kh]], axis=0)
        top = jnp.broadcast_to(high, (vecs, 128)) > 0.5
        lhs_ref[0:vecs, cols] = jnp.where(top, 0.0, data).astype(BF16)
        lhs_ref[vecs:2 * vecs, cols] = jnp.where(top, data, 0.0).astype(BF16)
    summed = dot_nt(lhs_ref[...], hot_ref[...]).astype(BF16)
    halves = []
    for h in range(2):
        blocks = []
        for c in range(2):
            rhs = summed[h * vecs:(h + 1) * vecs, c * 128:(c + 1) * 128]
            blocks.append(dot_nt(rhs, inv_ref[2 * h + c]))
        halves.append(jnp.concatenate(blocks, axis=1))
    solved = jnp.concatenate(halves, axis=0).astype(BF16)
    chunk = 1024
    for c in range(senders * 64 // chunk):
        found = dot_nn(solved, hot_ref[:, pl.ds(c * chunk, chunk)])
        for i in range(chunk // 128):
            lanes = slice(i * 128, (i + 1) * 128)
            j = c * (chunk // 128) + i
            top = jnp.broadcast_to(high_ref[0:1, pl.ds(j * 128, 128)], (vecs, 128)) > 0.5
            reply = jnp.where(top, found[vecs:, lanes], found[:vecs, lanes])
            even, odd = swap_pair(reply[:kh], reply[kh:])
            out_ref[2 * j] = even.astype(BF16)
            out_ref[2 * j + 1] = odd.astype(BF16)


def back_kernel(
    live_ref, ret_ref, dest_ref, local_ref, ires_ref, inv_hbm, cpl_hbm,
    inner_ref, face_ref,
    inv_ref, cpl_ref, lhs_ref, sem,
):
    subs, vecs, inner = ires_ref.shape
    face = face_ref.shape[2]
    kh = vecs // 2
    loads = []
    for s in range(subs):
        one = pltpu.make_async_copy(inv_hbm.at[s], inv_ref.at[s], sem.at[0, s])
        two = pltpu.make_async_copy(cpl_hbm.at[s], cpl_ref.at[s], sem.at[1, s])
        one.start()
        two.start()
        loads.append((one, two))
    senders = ret_ref.shape[0]
    wide = lhs_ref.shape[1]
    groups = lhs_ref.shape[0] // vecs
    pairs = wide // 128
    for j in range(senders // 2):
        first = ret_ref[2 * j].astype(F32)
        second = ret_ref[2 * j + 1].astype(F32)
        even, odd = swap_pair(first, second)
        a, i = j // pairs, j % pairs
        lhs_ref[a * vecs:a * vecs + kh, i * 128:(i + 1) * 128] = even.astype(BF16)
        lhs_ref[a * vecs + kh:(a + 1) * vecs, i * 128:(i + 1) * 128] = odd.astype(BF16)
    shift = wide.bit_length() - 1
    for s in range(subs):
        dest = dest_ref[:, pl.ds(s * face, face)]
        group = lax.shift_right_logical(dest, shift)
        within = jnp.bitwise_and(dest, wide - 1)
        hot = jnp.concatenate([one_hot(256, within - 256 * g) for g in range(wide // 256)], axis=0)
        found = dot_nn(lhs_ref[...], hot)
        group_all = jnp.broadcast_to(group, (vecs, face))
        correction = jnp.zeros((vecs, face), F32)
        for a in range(groups):
            correction = jnp.where(group_all == a, found[a * vecs:(a + 1) * vecs], correction)
        alive = lax.broadcasted_iota(jnp.int32, (vecs, face), 1) < live_ref[s]
        update = jnp.where(alive, local_ref[s] + correction, 0.0).astype(BF16)
        face_ref[s] = update
        loads[s][0].wait()
        loads[s][1].wait()
        extended = (ires_ref[s].astype(F32) - dot_nn(update, cpl_ref[s])).astype(BF16)
        inner_ref[s] = dot_nt(extended, inv_ref[s]).astype(BF16)


def vmem(count):
    return [pl.BlockSpec(memory_space=VMEM)] * count


ANY = pl.BlockSpec(memory_space=pl.ANY)
SMEM = pl.BlockSpec(memory_space=pltpu.SMEM)


def on_device(
    interior_res,
    interface_res,
    interior_inv,
    coupling,
    schur_inv,
    coarse_inv,
    coarse_part,
    coarse_slot,
    live_count,
):
    subs, vecs, inner = interior_res.shape
    face = interface_res.shape[2]
    rows = subs * face
    sections = lax.axis_size("sub") * lax.axis_size("grp")
    kh = vecs // 2
    groups = sections // 4
    shape = jax.ShapeDtypeStruct

    condensed, outgoing, dest = pl.pallas_call(
        front_kernel,
        name="front",
        out_shape=(
            shape((subs, vecs, face), BF16),
            shape((sections, kh + 8, 128), BF16),
            shape((1, rows), jnp.int32),
        ),
        in_specs=[SMEM] + vmem(4) + [ANY, ANY],
        out_specs=tuple(vmem(3)),
        scratch_shapes=[
            VMEM((subs, inner, inner), BF16),
            VMEM((subs, face, inner), BF16),
            VMEM((groups * (vecs + 2), face), BF16),
            VMEM((groups * (vecs + 2), 256), F32),
            pltpu.SemaphoreType.DMA((2, subs)),
        ],
        cost_estimate=pl.CostEstimate(flops=3 * 10**9, bytes_accessed=5 * 10**6, transcendentals=0),
    )(
        live_count, coarse_part.reshape(1, rows), coarse_slot.reshape(1, rows),
        interior_res, interface_res, interior_inv, coupling,
    )

    received = lax.all_to_all(outgoing, AXES, split_axis=0, concat_axis=0, tiled=True)

    local = pl.pallas_call(
        local_kernel,
        name="local",
        grid=(subs,),
        out_shape=shape((subs, vecs, face), F32),
        in_specs=[
            pl.BlockSpec((1, face, face), lambda s: (s, 0, 0)),
            pl.BlockSpec((1, vecs, face), lambda s: (s, 0, 0)),
        ],
        out_specs=pl.BlockSpec((1, vecs, face), lambda s: (s, 0, 0)),
        cost_estimate=pl.CostEstimate(
            flops=2 * rows * vecs * face, bytes_accessed=5 * 10**6, transcendentals=0
        ),
    )(schur_inv, condensed)

    blocks = coarse_inv.shape[0] // lax.axis_size("sub")
    mine = lax.dynamic_slice_in_dim(coarse_inv, lax.axis_index("sub") * blocks, blocks, 0)
    replies = pl.pallas_call(
        middle_kernel,
        name="middle",
        out_shape=shape((sections, kh, 128), BF16),
        in_specs=vmem(2),
        out_specs=vmem(1)[0],
        scratch_shapes=[
            VMEM((2 * vecs, sections * CAP), BF16),
            VMEM((256, sections * CAP), BF16),
            VMEM((8, sections * CAP), F32),
        ],
        cost_estimate=pl.CostEstimate(flops=10**9, bytes_accessed=2 * 10**6, transcendentals=0),
    )(received, mine)

    returned = lax.all_to_all(replies, AXES, split_axis=0, concat_axis=0, tiled=True)

    return pl.pallas_call(
        back_kernel,
        name="back",
        out_shape=(shape((subs, vecs, inner), BF16), shape((subs, vecs, face), BF16)),
        in_specs=[SMEM] + vmem(4) + [ANY, ANY],
        out_specs=tuple(vmem(2)),
        scratch_shapes=[
            VMEM((subs, inner, inner), BF16),
            VMEM((subs, face, inner), BF16),
            VMEM((8 * vecs, sections * CAP // 8), BF16),
            pltpu.SemaphoreType.DMA((2, subs)),
        ],
        cost_estimate=pl.CostEstimate(flops=3 * 10**9, bytes_accessed=6 * 10**6, transcendentals=0),
    )(live_count, returned, dest, local, interior_res, interior_inv, coupling)


def solution(mesh):
    rows = P(AXES)
    in_specs = (rows, rows, rows, rows, rows, P("grp"), rows, rows, rows)
    return jax.shard_map(
        on_device, mesh=mesh, in_specs=in_specs, out_specs=(rows, rows), check_vma=False
    )
```

```python
import jax
import jax.numpy as jnp
from jax import lax
from jax.experimental import pallas as pl
from jax.experimental.pallas import tpu as pltpu
from jax.sharding import PartitionSpec as P

F32 = jnp.float32
BF16 = jnp.bfloat16
AXES = ("sub", "grp")
CAP = 64
VMEM = pltpu.VMEM
HALF = 64


def dot_nn(left, right):
    return lax.dot_general(left, right, (((1,), (0,)), ((), ())), preferred_element_type=F32)


def dot_nt(left, right):
    return lax.dot_general(left, right, (((1,), (1,)), ((), ())), preferred_element_type=F32)


def low_half(rows):
    return lax.broadcasted_iota(jnp.int32, (rows, 128), 1).astype(BF16) < HALF


def turn(tile):
    return jnp.concatenate([tile[:, HALF:], tile[:, :HALF]], axis=1)


def one_hot(count, index):
    shape = (count, index.shape[1])
    rows = lax.broadcasted_iota(jnp.int32, shape, 0).astype(BF16)
    wanted = jnp.broadcast_to(index.astype(BF16), shape)
    return jnp.where(rows == wanted, jnp.ones(shape, BF16), jnp.zeros(shape, BF16))


def front_kernel(
    live_ref, part_ref, slot_ref, ires_ref, fres_ref, inv_hbm, cpl_hbm,
    cond_ref, out_ref, dest_ref,
    inv_ref, cpl_ref, mark_ref, own_ref, lhs_ref, hot_ref, acc_ref, sem,
):
    subs, vecs, inner = ires_ref.shape
    face = fres_ref.shape[2]
    loads = []
    for s in range(subs):
        one = pltpu.make_async_copy(inv_hbm.at[s], inv_ref.at[s], sem.at[0, s])
        two = pltpu.make_async_copy(cpl_hbm.at[s], cpl_ref.at[s], sem.at[1, s])
        one.start()
        two.start()
        loads.append((one, two))

    width = 256
    sections = out_ref.shape[0]
    chunks = subs * face // width
    row = lax.broadcasted_iota(jnp.int32, (2 * width, width), 0)
    column = lax.broadcasted_iota(jnp.int32, (2 * width, width), 1)
    counter = jnp.where(row - width <= column, 1.0, 0.0).astype(BF16)
    earlier = jnp.zeros((sections, width), BF16)
    for c in range(chunks):
        hot = one_hot(sections, part_ref[:, pl.ds(c * width, width)])
        block = pl.ds(c * sections, sections)
        mark_ref[block, 0:width] = earlier
        mark_ref[block, width:2 * width] = hot
        earlier = earlier + hot
    counted = dot_nn(mark_ref[...], counter).astype(BF16)
    own_ref[...] = jnp.where(mark_ref[:, width:2 * width] > 0, counted, jnp.zeros_like(counted))
    chunk_row = lax.broadcasted_iota(jnp.int32, (chunks, chunks * sections), 0)
    chunk_of = lax.broadcasted_iota(jnp.int32, (chunks, chunks * sections), 1) // sections
    place = dot_nn(jnp.where(chunk_row == chunk_of, 1.0, 0.0).astype(BF16), own_ref[...])
    place = place.astype(jnp.int32) - 1
    for c in range(chunks):
        cols = pl.ds(c * width, width)
        dest_ref[:, cols] = part_ref[:, cols] * CAP + place[c:c + 1]

    groups = sections // 4
    base = groups * vecs
    for s in range(subs):
        loads[s][0].wait()
        loads[s][1].wait()
        pre = dot_nt(ires_ref[s], inv_ref[s]).astype(BF16)
        cond = fres_ref[s].astype(F32) - dot_nt(pre, cpl_ref[s])
        alive = lax.broadcasted_iota(jnp.int32, (vecs, face), 1) < live_ref[s]
        cond = jnp.where(alive, cond, 0.0).astype(BF16)
        cond_ref[s] = cond
        cols = pl.ds(s * face, face)
        dest = dest_ref[:, cols]
        hot_ref[:, cols] = one_hot(256, jnp.bitwise_and(dest, 255))
        group = lax.shift_right_logical(dest, 8).astype(BF16)
        group_all = jnp.broadcast_to(group, (vecs, face))
        for a in range(groups):
            lhs_ref[a * vecs:(a + 1) * vecs, cols] = jnp.where(group_all == a, cond, jnp.zeros_like(cond))
        slot = slot_ref[:, cols]
        mine = one_hot(groups, group)
        high = jnp.broadcast_to(lax.shift_right_logical(slot, 7).astype(BF16), (groups, face))
        low = jnp.broadcast_to(jnp.bitwise_and(slot, 127).astype(BF16), (groups, face))
        lhs_ref[base:base + groups, cols] = mine * high
        lhs_ref[base + groups:base + 2 * groups, cols] = mine * low
        if (s + 1) % 1 == 0:
            span = pl.ds((s + 1 - 1) * face, 1 * face)
            part = dot_nt(lhs_ref[:, span], hot_ref[:, span])
            acc_ref[...] = part if s < 1 else acc_ref[...] + part

    kh = vecs // 2
    mask = low_half(kh)
    mask_wide = low_half(groups)
    first_row = lax.broadcasted_iota(jnp.int32, (8, 128), 0) == 0
    for h in range(2):
        lanes = pl.ds(h * 128, 128)
        slots = []
        for i in range(2):
            value = acc_ref[pl.ds(base + i * groups, groups), lanes].astype(BF16)
            turned = turn(value)
            slots.append((
                jnp.where(mask_wide, value, turned).astype(F32),
                jnp.where(mask_wide, turned, value).astype(F32),
            ))
        for a in range(groups):
            first = acc_ref[pl.ds(a * vecs, kh), lanes].astype(BF16)
            second = turn(acc_ref[pl.ds(a * vecs + kh, kh), lanes].astype(BF16))
            p = 4 * a + 2 * h
            out_ref[p, 0:kh, :] = jnp.where(mask, first, second)
            out_ref[p + 1, 0:kh, :] = jnp.where(mask, second, first)
            for i in range(2):
                both = jnp.where(
                    first_row,
                    jnp.broadcast_to(slots[0][i][a:a + 1], (8, 128)),
                    jnp.broadcast_to(slots[1][i][a:a + 1], (8, 128)),
                )
                out_ref[p + i, kh:kh + 8, :] = both.astype(BF16)


def local_kernel(schur_ref, cond_ref, out_ref):
    out_ref[0] = dot_nt(cond_ref[0], schur_ref[0])


def middle_kernel(recv_ref, inv_ref, out_ref, lhs_ref, hot_ref, high_ref):
    senders = recv_ref.shape[0]
    kh = out_ref.shape[1]
    vecs = 2 * kh
    blocks = inv_ref.shape[0]
    mask = low_half(kh)
    zero = jnp.zeros((kh, 128), BF16)
    for j in range(senders // 2):
        cols = pl.ds(j * 128, 128)
        first = recv_ref[2 * j, 0:kh, :]
        second = recv_ref[2 * j + 1, 0:kh, :]
        data = (jnp.where(mask, first, turn(second)), jnp.where(mask, turn(first), second))
        slots = jnp.where(
            mask[:8],
            recv_ref[2 * j, kh:kh + 8, :],
            recv_ref[2 * j + 1, kh:kh + 8, :],
        )
        hot_ref[:, cols] = one_hot(128, slots[1:2])
        high = jnp.broadcast_to(slots[0:1], (kh, 128))
        high_ref[:, cols] = high
        for c in range(blocks):
            here = high == c
            for i in range(2):
                at = c * vecs + i * kh
                lhs_ref[at:at + kh, cols] = jnp.where(here, data[i], zero)
    summed = dot_nt(lhs_ref[...], hot_ref[...]).astype(BF16)
    solved = jnp.concatenate(
        [dot_nt(summed[c * vecs:(c + 1) * vecs], inv_ref[c]) for c in range(blocks)], axis=0
    ).astype(BF16)
    chunk = 1024
    for n in range(senders * CAP // chunk):
        found = dot_nn(solved, hot_ref[:, pl.ds(n * chunk, chunk)])
        for i in range(chunk // 128):
            lanes = slice(i * 128, (i + 1) * 128)
            j = n * (chunk // 128) + i
            high = high_ref[:, pl.ds(j * 128, 128)]
            parts = []
            for t in range(2):
                part = zero
                for c in range(blocks):
                    at = c * vecs + t * kh
                    part = jnp.where(high == c, found[at:at + kh, lanes].astype(BF16), part)
                parts.append(part)
            out_ref[2 * j] = jnp.where(mask, parts[0], turn(parts[1]))
            out_ref[2 * j + 1] = jnp.where(mask, turn(parts[0]), parts[1])


def back_kernel(
    live_ref, ret_ref, dest_ref, local_ref, ires_ref, inv_hbm, cpl_hbm,
    inner_ref, face_ref,
    inv_ref, cpl_ref, lhs_ref, sem,
):
    subs, vecs, inner = ires_ref.shape
    face = face_ref.shape[2]
    kh = vecs // 2
    loads = []
    for s in range(subs):
        one = pltpu.make_async_copy(inv_hbm.at[s], inv_ref.at[s], sem.at[0, s])
        two = pltpu.make_async_copy(cpl_hbm.at[s], cpl_ref.at[s], sem.at[1, s])
        one.start()
        two.start()
        loads.append((one, two))
    senders = ret_ref.shape[0]
    wide = lhs_ref.shape[1]
    groups = lhs_ref.shape[0] // vecs
    pairs = wide // 128
    mask = low_half(kh)
    for j in range(senders // 2):
        first = ret_ref[2 * j]
        second = ret_ref[2 * j + 1]
        a, i = j // pairs, j % pairs
        lanes = slice(i * 128, (i + 1) * 128)
        lhs_ref[a * vecs:a * vecs + kh, lanes] = jnp.where(mask, first, second)
        lhs_ref[a * vecs + kh:(a + 1) * vecs, lanes] = turn(jnp.where(mask, second, first))
    shift = wide.bit_length() - 1
    for s in range(subs):
        dest = dest_ref[:, pl.ds(s * face, face)]
        group = lax.shift_right_logical(dest, shift)
        within = jnp.bitwise_and(dest, wide - 1)
        hot = jnp.concatenate([one_hot(256, within - 256 * g) for g in range(wide // 256)], axis=0)
        found = dot_nn(lhs_ref[...], hot)
        group_all = jnp.broadcast_to(group, (vecs, face))
        correction = jnp.zeros((vecs, face), F32)
        for a in range(groups):
            correction = jnp.where(group_all == a, found[a * vecs:(a + 1) * vecs], correction)
        alive = lax.broadcasted_iota(jnp.int32, (vecs, face), 1) < live_ref[s]
        update = jnp.where(alive, local_ref[s] + correction, 0.0).astype(BF16)
        face_ref[s] = update
        loads[s][0].wait()
        loads[s][1].wait()
        extended = (ires_ref[s].astype(F32) - dot_nn(update, cpl_ref[s])).astype(BF16)
        inner_ref[s] = dot_nt(extended, inv_ref[s]).astype(BF16)


def vmem(count):
    return [pl.BlockSpec(memory_space=VMEM)] * count


HBM = pl.BlockSpec(memory_space=pltpu.HBM)
SMEM = pl.BlockSpec(memory_space=pltpu.SMEM)


def on_device(
    interior_res,
    interface_res,
    interior_inv,
    coupling,
    schur_inv,
    coarse_inv,
    coarse_part,
    coarse_slot,
    live_count,
):
    subs, vecs, inner = interior_res.shape
    face = interface_res.shape[2]
    rows = subs * face
    sections = lax.axis_size("sub") * lax.axis_size("grp")
    kh = vecs // 2
    groups = sections // 4
    shape = jax.ShapeDtypeStruct

    condensed, outgoing, dest = pl.pallas_call(
        front_kernel,
        name="front",
        out_shape=(
            shape((subs, vecs, face), BF16),
            shape((sections, kh + 8, 128), BF16),
            shape((1, rows), jnp.int32),
        ),
        in_specs=[SMEM] + vmem(4) + [HBM, HBM],
        out_specs=tuple(vmem(3)),
        scratch_shapes=[
            VMEM((subs, inner, inner), BF16),
            VMEM((subs, face, inner), BF16),
            VMEM((rows // 256 * sections, 512), BF16),
            VMEM((rows // 256 * sections, 256), BF16),
            VMEM((groups * (vecs + 2), rows), BF16),
            VMEM((256, rows), BF16),
            VMEM((groups * (vecs + 2), 256), F32),
            pltpu.SemaphoreType.DMA((2, subs)),
        ],
        cost_estimate=pl.CostEstimate(flops=3 * 10**9, bytes_accessed=5 * 10**6, transcendentals=0),
    )(
        live_count, coarse_part.reshape(1, rows), coarse_slot.reshape(1, rows),
        interior_res, interface_res, interior_inv, coupling,
    )

    received = lax.all_to_all(outgoing, AXES, split_axis=0, concat_axis=0, tiled=True)

    local = pl.pallas_call(
        local_kernel,
        name="local",
        compiler_params=pltpu.CompilerParams(vmem_limit_bytes=52 * 2**20),
        grid=(subs,),
        out_shape=shape((subs, vecs, face), F32),
        in_specs=[
            pl.BlockSpec((1, face, face), lambda s: (s, 0, 0)),
            pl.BlockSpec((1, vecs, face), lambda s: (s, 0, 0)),
        ],
        out_specs=pl.BlockSpec((1, vecs, face), lambda s: (s, 0, 0)),
        cost_estimate=pl.CostEstimate(
            flops=2 * rows * vecs * face, bytes_accessed=5 * 10**6, transcendentals=0
        ),
    )(schur_inv, condensed)

    blocks = coarse_inv.shape[0] // lax.axis_size("sub")
    mine = lax.dynamic_slice_in_dim(coarse_inv, lax.axis_index("sub") * blocks, blocks, 0)
    replies = pl.pallas_call(
        middle_kernel,
        name="middle",
        compiler_params=pltpu.CompilerParams(vmem_limit_bytes=24 * 2**20),
        out_shape=shape((sections, kh, 128), BF16),
        in_specs=vmem(2),
        out_specs=vmem(1)[0],
        scratch_shapes=[
            VMEM((blocks * vecs, sections * CAP), BF16),
            VMEM((128, sections * CAP), BF16),
            VMEM((kh, sections * CAP), BF16),
        ],
        cost_estimate=pl.CostEstimate(flops=10**9, bytes_accessed=2 * 10**6, transcendentals=0),
    )(received, mine)

    returned = lax.all_to_all(replies, AXES, split_axis=0, concat_axis=0, tiled=True)

    return pl.pallas_call(
        back_kernel,
        name="back",
        compiler_params=pltpu.CompilerParams(vmem_limit_bytes=52 * 2**20),
        out_shape=(shape((subs, vecs, inner), BF16), shape((subs, vecs, face), BF16)),
        in_specs=[SMEM] + vmem(4) + [HBM, HBM],
        out_specs=tuple(vmem(2)),
        scratch_shapes=[
            VMEM((subs, inner, inner), BF16),
            VMEM((subs, face, inner), BF16),
            VMEM((16 * vecs, sections * CAP // 16), BF16),
            pltpu.SemaphoreType.DMA((2, subs)),
        ],
        cost_estimate=pl.CostEstimate(flops=3 * 10**9, bytes_accessed=6 * 10**6, transcendentals=0),
    )(live_count, returned, dest, local, interior_res, interior_inv, coupling)


def solution(mesh):
    rows = P(AXES)
    in_specs = (rows, rows, rows, rows, rows, P("grp"), rows, rows, rows)
    return jax.shard_map(
        on_device, mesh=mesh, in_specs=in_specs, out_specs=(rows, rows), check_vma=False
    )
```

```python
import jax
import jax.numpy as jnp
from jax import lax
from jax.experimental import pallas as pl
from jax.experimental.pallas import tpu as pltpu
from jax.sharding import PartitionSpec as P

F32 = jnp.float32
BF16 = jnp.bfloat16
AXES = ("sub", "grp")
CAP = 64
VMEM = pltpu.VMEM
HALF = 64


def dot_nn(left, right):
    return lax.dot_general(left, right, (((1,), (0,)), ((), ())), preferred_element_type=F32)


def dot_nt(left, right):
    return lax.dot_general(left, right, (((1,), (1,)), ((), ())), preferred_element_type=F32)


def low_half(rows):
    return lax.broadcasted_iota(jnp.int32, (rows, 128), 1).astype(BF16) < HALF


def turn(tile):
    return jnp.concatenate([tile[:, HALF:], tile[:, :HALF]], axis=1)


def swap_pair(first, second):
    mask = lax.broadcasted_iota(jnp.int32, first.shape, 1) < HALF
    even = jnp.where(mask, first, pltpu.roll(second, HALF, 1))
    odd = jnp.where(mask, pltpu.roll(first, HALF, 1), second)
    return even, odd


def one_hot(count, index):
    shape = (count, index.shape[1])
    rows = lax.broadcasted_iota(jnp.int32, shape, 0).astype(BF16)
    wanted = jnp.broadcast_to(index.astype(BF16), shape)
    return jnp.where(rows == wanted, jnp.ones(shape, BF16), jnp.zeros(shape, BF16))


def front_kernel(
    live_ref, part_ref, slot_ref, ires_hbm, fres_hbm, inv_hbm, cpl_hbm,
    cond_hbm, out_hbm, dest_ref,
    ires_ref, fres_ref, inv_ref, cpl_ref, mark_ref, own_ref, cond_ref, lhs_ref, hot_ref, mark_slot_ref, place_ref, out_ref,
    sem, res_sem, out_sem, cond_sem,
):
    subs, vecs, inner = ires_ref.shape
    face = fres_ref.shape[2]
    residuals = [
        pltpu.make_async_copy(ires_hbm, ires_ref, res_sem.at[0]),
        pltpu.make_async_copy(fres_hbm, fres_ref, res_sem.at[1]),
    ]
    loads = []
    for copy in residuals:
        copy.start()
    for s in range(subs):
        one = pltpu.make_async_copy(inv_hbm.at[s], inv_ref.at[s], sem.at[0, s])
        two = pltpu.make_async_copy(cpl_hbm.at[s], cpl_ref.at[s], sem.at[1, s])
        loads.append((one, two))
    for i in range(2):
        for s in range(subs):
            loads[s][i].start()

    width = 256
    sections = out_ref.shape[0]
    chunks = subs * face // width
    row = lax.broadcasted_iota(jnp.int32, (2 * width, width), 0)
    column = lax.broadcasted_iota(jnp.int32, (2 * width, width), 1)
    counter = jnp.where(row - width <= column, 1.0, 0.0).astype(BF16)
    earlier = jnp.zeros((sections, width), BF16)
    for c in range(chunks):
        hot = one_hot(sections, part_ref[:, pl.ds(c * width, width)])
        block = pl.ds(c * sections, sections)
        mark_ref[block, 0:width] = earlier
        mark_ref[block, width:2 * width] = hot
        earlier = earlier + hot
    counted = dot_nn(mark_ref[...], counter).astype(BF16)
    own_ref[...] = jnp.where(mark_ref[:, width:2 * width] > 0, counted, jnp.zeros_like(counted))
    chunk_row = lax.broadcasted_iota(jnp.int32, (chunks, chunks * sections), 0)
    chunk_of = lax.broadcasted_iota(jnp.int32, (chunks, chunks * sections), 1) // sections
    place = dot_nn(jnp.where(chunk_row == chunk_of, 1.0, 0.0).astype(BF16), own_ref[...])
    place = place.astype(jnp.int32) - 1
    for c in range(chunks):
        cols = pl.ds(c * width, width)
        dest_ref[:, cols] = part_ref[:, cols] * CAP + place[c:c + 1]
    quads = sections // 4
    for s in range(subs):
        cols = pl.ds(s * face, face)
        dest = dest_ref[:, cols]
        hot_ref[:, cols] = one_hot(256, jnp.bitwise_and(dest, 255))
        mine = one_hot(quads, lax.shift_right_logical(dest, 8))
        slot = slot_ref[:, cols]
        high = lax.shift_right_logical(slot, 7).astype(BF16)
        low = jnp.bitwise_and(slot, 127).astype(BF16)
        mark_slot_ref[0:quads, cols] = mine * jnp.broadcast_to(high, mine.shape)
        mark_slot_ref[quads:2 * quads, cols] = mine * jnp.broadcast_to(low, mine.shape)
    slots = dot_nt(mark_slot_ref[...], hot_ref[...])
    for h in range(2):
        lanes = slice(h * 128, (h + 1) * 128)
        even, odd = swap_pair(slots[0:quads, lanes], slots[quads:2 * quads, lanes])
        place_ref[0:quads, lanes] = even
        place_ref[quads:2 * quads, lanes] = odd

    @pl.when(live_ref[0] >= 0)
    def _():
        for copy in residuals:
            copy.wait()
        for s in range(subs):
            loads[s][0].wait()
        pres = [dot_nt(ires_ref[s], inv_ref[s]).astype(BF16) for s in range(subs)]
        for s in range(subs):
            loads[s][1].wait()
        for s in range(subs):
            cond = fres_ref[s].astype(F32) - dot_nt(pres[s], cpl_ref[s])
            alive = lax.broadcasted_iota(jnp.int32, (vecs, face), 1) < live_ref[s]
            cond_ref[s] = jnp.where(alive, cond, 0.0).astype(BF16)
    keep = pltpu.make_async_copy(cond_ref, cond_hbm, cond_sem)
    keep.start()

    groups = 8
    kh = vecs // 2
    mask = low_half(kh)
    stores = []
    for block in range(quads // groups):
        buf = block % 2
        for s in range(subs):
            cols = pl.ds(s * face, face)
            cond = cond_ref[s]
            group = lax.shift_right_logical(dest_ref[:, cols], 8).astype(BF16) - block * groups
            group_all = jnp.broadcast_to(group, (vecs, face))
            for a in range(groups):
                lhs_ref[buf, a * vecs:(a + 1) * vecs, cols] = jnp.where(
                    group_all == a, cond, jnp.zeros_like(cond)
                )
        acc = dot_nt(lhs_ref[buf], hot_ref[...])
        for h in range(2):
            lanes = slice(h * 128, (h + 1) * 128)
            for a in range(groups):
                first = acc[a * vecs:a * vecs + kh, lanes].astype(BF16)
                second = turn(acc[a * vecs + kh:(a + 1) * vecs, lanes].astype(BF16))
                p = 4 * (block * groups + a) + 2 * h
                out_ref[p, 0:kh, :] = jnp.where(mask, first, second)
                out_ref[p + 1, 0:kh, :] = jnp.where(mask, second, first)
                q = block * groups + a
                for i in range(2):
                    value = place_ref[q + i * quads:q + i * quads + 1, lanes]
                    out_ref[p + i, kh:kh + 8, :] = jnp.broadcast_to(value, (8, 128)).astype(BF16)
        span = pl.ds(block * 4 * groups, 4 * groups)
        store = pltpu.make_async_copy(out_ref.at[span], out_hbm.at[span], out_sem.at[block])
        store.start()
        stores.append(store)
    keep.wait()
    for store in stores:
        store.wait()


def local_kernel(cond_ref, schur_hbm, local_ref, schur_ref, sem):
    subs = cond_ref.shape[0]
    loads = [pltpu.make_async_copy(schur_hbm.at[s], schur_ref.at[s], sem.at[s]) for s in range(subs)]
    for copy in loads:
        copy.start()
    for s in range(subs):
        loads[s].wait()
        local_ref[s] = dot_nt(cond_ref[s], schur_ref[s])


def middle_kernel(recv_ref, inv_ref, out_ref, lhs_ref, hot_ref, high_ref):
    senders = recv_ref.shape[0]
    kh = out_ref.shape[1]
    vecs = 2 * kh
    blocks = inv_ref.shape[0]
    mask = low_half(kh)
    zero = jnp.zeros((kh, 128), BF16)
    for j in range(senders // 2):
        cols = pl.ds(j * 128, 128)
        first = recv_ref[2 * j, 0:kh, :]
        second = recv_ref[2 * j + 1, 0:kh, :]
        data = (jnp.where(mask, first, turn(second)), jnp.where(mask, turn(first), second))
        first = recv_ref[2 * j, kh:kh + 8, :]
        second = recv_ref[2 * j + 1, kh:kh + 8, :]
        hot_ref[:, cols] = one_hot(128, jnp.where(mask[:8], turn(first), second)[0:1])
        high = jnp.broadcast_to(jnp.where(mask[:8], first, turn(second))[0:1], (kh, 128))
        high_ref[:, cols] = high
        for c in range(blocks):
            here = high == c
            for i in range(2):
                at = c * vecs + i * kh
                lhs_ref[at:at + kh, cols] = jnp.where(here, data[i], zero)
    summed = dot_nt(lhs_ref[...], hot_ref[...]).astype(BF16)
    solved = jnp.concatenate(
        [dot_nt(summed[c * vecs:(c + 1) * vecs], inv_ref[c]) for c in range(blocks)], axis=0
    ).astype(BF16)
    chunk = 1024
    for n in range(senders * CAP // chunk):
        found = dot_nn(solved, hot_ref[:, pl.ds(n * chunk, chunk)])
        for i in range(chunk // 128):
            lanes = slice(i * 128, (i + 1) * 128)
            j = n * (chunk // 128) + i
            high = high_ref[:, pl.ds(j * 128, 128)]
            parts = []
            for t in range(2):
                part = zero
                for c in range(blocks):
                    at = c * vecs + t * kh
                    part = jnp.where(high == c, found[at:at + kh, lanes].astype(BF16), part)
                parts.append(part)
            out_ref[2 * j] = jnp.where(mask, parts[0], turn(parts[1]))
            out_ref[2 * j + 1] = jnp.where(mask, turn(parts[0]), parts[1])


def back_kernel(
    live_ref, ret_ref, dest_ref, ires_ref, local_hbm, inv_hbm, cpl_hbm,
    inner_hbm, face_hbm,
    local_ref, inv_ref, cpl_ref, lhs_ref, hot_ref, inner_ref, face_ref, sem, out_sem,
):
    subs, vecs, inner = ires_ref.shape
    face = face_ref.shape[2]
    kh = vecs // 2
    loads = [
        pltpu.make_async_copy(local_hbm, local_ref, sem.at[0]),
        pltpu.make_async_copy(cpl_hbm, cpl_ref, sem.at[1]),
        pltpu.make_async_copy(inv_hbm, inv_ref, sem.at[2]),
    ]
    stores = [
        pltpu.make_async_copy(face_ref, face_hbm, out_sem.at[0]),
        pltpu.make_async_copy(inner_ref, inner_hbm, out_sem.at[1]),
    ]
    for copy in loads:
        copy.start()
    senders = ret_ref.shape[0]
    wide = lhs_ref.shape[1]
    groups = lhs_ref.shape[0] // vecs
    pairs = wide // 128
    mask = low_half(kh)
    for j in range(senders // 2):
        first = ret_ref[2 * j]
        second = ret_ref[2 * j + 1]
        a, i = j // pairs, j % pairs
        lanes = slice(i * 128, (i + 1) * 128)
        lhs_ref[a * vecs:a * vecs + kh, lanes] = jnp.where(mask, first, second)
        lhs_ref[a * vecs + kh:(a + 1) * vecs, lanes] = turn(jnp.where(mask, second, first))
    loads[0].wait()
    shift = wide.bit_length() - 1
    for s in range(subs):
        cols = pl.ds(s * face, face)
        dest = dest_ref[:, cols]
        within = jnp.bitwise_and(dest, wide - 1)
        for g in range(wide // 256):
            hot_ref[s, pl.ds(g * 256, 256), :] = one_hot(256, within - 256 * g)
        found = dot_nn(lhs_ref[...], hot_ref[s])
        group_all = jnp.broadcast_to(lax.shift_right_logical(dest, shift), (vecs, face))
        correction = jnp.zeros((vecs, face), F32)
        for a in range(groups):
            correction = jnp.where(group_all == a, found[a * vecs:(a + 1) * vecs], correction)
        alive = lax.broadcasted_iota(jnp.int32, (vecs, face), 1) < live_ref[s]
        face_ref[s] = jnp.where(alive, local_ref[s] + correction, 0.0).astype(BF16)
    stores[0].start()
    for copy in loads[1:]:
        copy.wait()
    extended = [
        (ires_ref[s].astype(F32) - dot_nn(face_ref[s], cpl_ref[s])).astype(BF16) for s in range(subs)
    ]
    for s in range(subs):
        inner_ref[s] = dot_nt(extended[s], inv_ref[s]).astype(BF16)
    stores[1].start()
    for copy in stores:
        copy.wait()


def vmem(count):
    return [pl.BlockSpec(memory_space=VMEM)] * count


HBM = pl.BlockSpec(memory_space=pltpu.HBM)
SMEM = pl.BlockSpec(memory_space=pltpu.SMEM)


def on_device(
    interior_res,
    interface_res,
    interior_inv,
    coupling,
    schur_inv,
    coarse_inv,
    coarse_part,
    coarse_slot,
    live_count,
):
    subs, vecs, inner = interior_res.shape
    face = interface_res.shape[2]
    rows = subs * face
    sections = lax.axis_size("sub") * lax.axis_size("grp")
    kh = vecs // 2
    groups = sections // 4
    shape = jax.ShapeDtypeStruct

    condensed, outgoing, dest = pl.pallas_call(
        front_kernel,
        name="front",
        out_shape=(
            shape((subs, vecs, face), BF16),
            shape((sections, kh + 8, 128), BF16),
            shape((1, rows), jnp.int32),
        ),
        in_specs=[SMEM] + vmem(2) + [HBM] * 4,
        out_specs=(HBM, HBM, vmem(1)[0]),
        scratch_shapes=[
            VMEM((subs, vecs, inner), BF16),
            VMEM((subs, vecs, face), BF16),
            VMEM((subs, inner, inner), BF16),
            VMEM((subs, face, inner), BF16),
            VMEM((rows // 256 * sections, 512), BF16),
            VMEM((rows // 256 * sections, 256), BF16),
            VMEM((subs, vecs, face), BF16),
            VMEM((2, 8 * vecs, rows), BF16),
            VMEM((256, rows), BF16),
            VMEM((sections // 2, rows), BF16),
            VMEM((sections // 2, 256), F32),
            VMEM((sections, kh + 8, 128), BF16),
            pltpu.SemaphoreType.DMA((2, subs)),
            pltpu.SemaphoreType.DMA((2,)),
            pltpu.SemaphoreType.DMA((sections // 32,)),
            pltpu.SemaphoreType.DMA(()),
        ],
        cost_estimate=pl.CostEstimate(flops=3 * 10**9, bytes_accessed=5 * 10**6, transcendentals=0),
    )(
        live_count, coarse_part.reshape(1, rows), coarse_slot.reshape(1, rows),
        interior_res, interface_res, interior_inv, coupling,
    )

    received = lax.all_to_all(outgoing, AXES, split_axis=0, concat_axis=0, tiled=True)

    local = pl.pallas_call(
        local_kernel,
        name="local",
        compiler_params=pltpu.CompilerParams(vmem_limit_bytes=56 * 2**20),
        out_shape=shape((subs, vecs, face), F32),
        in_specs=vmem(1) + [HBM],
        out_specs=vmem(1)[0],
        scratch_shapes=[VMEM((subs, face, face), BF16), pltpu.SemaphoreType.DMA((subs,))],
        cost_estimate=pl.CostEstimate(
            flops=2 * rows * vecs * face, bytes_accessed=5 * 10**6, transcendentals=0
        ),
    )(condensed, schur_inv)

    blocks = coarse_inv.shape[0] // lax.axis_size("sub")
    mine = lax.dynamic_slice_in_dim(coarse_inv, lax.axis_index("sub") * blocks, blocks, 0)
    replies = pl.pallas_call(
        middle_kernel,
        name="middle",
        compiler_params=pltpu.CompilerParams(vmem_limit_bytes=24 * 2**20),
        out_shape=shape((sections, kh, 128), BF16),
        in_specs=vmem(2),
        out_specs=vmem(1)[0],
        scratch_shapes=[
            VMEM((blocks * vecs, sections * CAP), BF16),
            VMEM((128, sections * CAP), BF16),
            VMEM((kh, sections * CAP), BF16),
        ],
        cost_estimate=pl.CostEstimate(flops=10**9, bytes_accessed=2 * 10**6, transcendentals=0),
    )(received, mine)

    returned = lax.all_to_all(replies, AXES, split_axis=0, concat_axis=0, tiled=True)

    return pl.pallas_call(
        back_kernel,
        name="back",
        compiler_params=pltpu.CompilerParams(vmem_limit_bytes=53 * 2**20),
        out_shape=(shape((subs, vecs, inner), BF16), shape((subs, vecs, face), BF16)),
        in_specs=[SMEM] + vmem(3) + [HBM] * 3,
        out_specs=(HBM, HBM),
        scratch_shapes=[
            VMEM((subs, vecs, face), F32),
            VMEM((subs, inner, inner), BF16),
            VMEM((subs, face, inner), BF16),
            VMEM((16 * vecs, sections * CAP // 16), BF16),
            VMEM((subs, sections * CAP // 16, face), BF16),
            VMEM((subs, vecs, inner), BF16),
            VMEM((subs, vecs, face), BF16),
            pltpu.SemaphoreType.DMA((3,)),
            pltpu.SemaphoreType.DMA((2,)),
        ],
        cost_estimate=pl.CostEstimate(flops=3 * 10**9, bytes_accessed=6 * 10**6, transcendentals=0),
    )(live_count, returned, dest, interior_res, local, interior_inv, coupling)


def solution(mesh):
    rows = P(AXES)
    in_specs = (rows, rows, rows, rows, rows, P("grp"), rows, rows, rows)
    return jax.shard_map(
        on_device, mesh=mesh, in_specs=in_specs, out_specs=(rows, rows), check_vma=False
    )
```

```python
import jax
import jax.numpy as jnp
from jax import lax
from jax.experimental import pallas as pl
from jax.experimental.pallas import tpu as pltpu
from jax.sharding import PartitionSpec as P

F32 = jnp.float32
BF16 = jnp.bfloat16
AXES = ("sub", "grp")
CAP = 64
VMEM = pltpu.VMEM
HALF = 64


def dot_nn(left, right):
    return lax.dot_general(left, right, (((1,), (0,)), ((), ())), preferred_element_type=F32)


def dot_nt(left, right):
    return lax.dot_general(left, right, (((1,), (1,)), ((), ())), preferred_element_type=F32)


def low_half(rows):
    return lax.broadcasted_iota(jnp.int32, (rows, 128), 1).astype(BF16) < HALF


def turn(tile):
    return jnp.concatenate([tile[:, HALF:], tile[:, :HALF]], axis=1)


def swap_pair(first, second):
    mask = lax.broadcasted_iota(jnp.int32, first.shape, 1) < HALF
    even = jnp.where(mask, first, pltpu.roll(second, HALF, 1))
    odd = jnp.where(mask, pltpu.roll(first, HALF, 1), second)
    return even, odd


def one_hot(count, index):
    shape = (count, index.shape[1])
    rows = lax.broadcasted_iota(jnp.int32, shape, 0).astype(BF16)
    wanted = jnp.broadcast_to(index.astype(BF16), shape)
    return jnp.where(rows == wanted, jnp.ones(shape, BF16), jnp.zeros(shape, BF16))


def front_kernel(
    live_ref, part_ref, slot_ref, ires_hbm, fres_hbm, inv_hbm, cpl_hbm,
    cond_hbm, out_hbm, dest_ref,
    ires_ref, fres_ref, inv_ref, cpl_ref, mark_ref, own_ref, cond_ref, lhs_ref, hot_ref, mark_slot_ref, place_ref, out_ref,
    sem, res_sem, out_sem, cond_sem,
):
    subs, vecs, inner = ires_ref.shape
    face = fres_ref.shape[2]
    residuals = [
        pltpu.make_async_copy(ires_hbm, ires_ref, res_sem.at[0]),
        pltpu.make_async_copy(fres_hbm, fres_ref, res_sem.at[1]),
    ]
    loads = []
    for copy in residuals:
        copy.start()
    for s in range(subs):
        one = pltpu.make_async_copy(inv_hbm.at[s], inv_ref.at[s], sem.at[0, s])
        two = pltpu.make_async_copy(cpl_hbm.at[s], cpl_ref.at[s], sem.at[1, s])
        loads.append((one, two))
    for i in range(2):
        for s in range(subs):
            loads[s][i].start()

    width = 256
    tall = vecs // 2 + 2
    sections = out_ref.shape[0] // tall
    chunks = subs * face // width
    row = lax.broadcasted_iota(jnp.int32, (2 * width, width), 0)
    column = lax.broadcasted_iota(jnp.int32, (2 * width, width), 1)
    counter = jnp.where(row - width <= column, 1.0, 0.0).astype(BF16)
    earlier = jnp.zeros((sections, width), BF16)
    for c in range(chunks):
        hot = one_hot(sections, part_ref[:, pl.ds(c * width, width)])
        block = pl.ds(c * sections, sections)
        mark_ref[block, 0:width] = earlier
        mark_ref[block, width:2 * width] = hot
        earlier = earlier + hot
    counted = dot_nn(mark_ref[...], counter).astype(BF16)
    own_ref[...] = jnp.where(mark_ref[:, width:2 * width] > 0, counted, jnp.zeros_like(counted))
    chunk_row = lax.broadcasted_iota(jnp.int32, (chunks, chunks * sections), 0)
    chunk_of = lax.broadcasted_iota(jnp.int32, (chunks, chunks * sections), 1) // sections
    place = dot_nn(jnp.where(chunk_row == chunk_of, 1.0, 0.0).astype(BF16), own_ref[...])
    place = place.astype(jnp.int32) - 1
    for c in range(chunks):
        cols = pl.ds(c * width, width)
        dest_ref[:, cols] = part_ref[:, cols] * CAP + place[c:c + 1]
    quads = sections // 4
    for s in range(subs):
        cols = pl.ds(s * face, face)
        dest = dest_ref[:, cols]
        hot_ref[:, cols] = one_hot(256, jnp.bitwise_and(dest, 255))
        mine = one_hot(quads, lax.shift_right_logical(dest, 8))
        slot = slot_ref[:, cols]
        high = lax.shift_right_logical(slot, 7).astype(BF16)
        low = jnp.bitwise_and(slot, 127).astype(BF16)
        mark_slot_ref[0:quads, cols] = mine * jnp.broadcast_to(high, mine.shape)
        mark_slot_ref[quads:2 * quads, cols] = mine * jnp.broadcast_to(low, mine.shape)
    slots = dot_nt(mark_slot_ref[...], hot_ref[...])
    for h in range(2):
        lanes = slice(h * 128, (h + 1) * 128)
        even, odd = swap_pair(slots[0:quads, lanes], slots[quads:2 * quads, lanes])
        place_ref[0:quads, lanes] = even
        place_ref[quads:2 * quads, lanes] = odd

    @pl.when(live_ref[0] >= 0)
    def _():
        for copy in residuals:
            copy.wait()
        for s in range(subs):
            loads[s][0].wait()
        pres = [dot_nt(ires_ref[s], inv_ref[s]).astype(BF16) for s in range(subs)]
        for s in range(subs):
            loads[s][1].wait()
        for s in range(subs):
            cond = fres_ref[s].astype(F32) - dot_nt(pres[s], cpl_ref[s])
            alive = lax.broadcasted_iota(jnp.int32, (vecs, face), 1) < live_ref[s]
            cond_ref[s] = jnp.where(alive, cond, 0.0).astype(BF16)
    keep = pltpu.make_async_copy(cond_ref, cond_hbm, cond_sem)
    keep.start()

    groups = 8
    kh = vecs // 2
    mask = low_half(kh)
    stores = []
    for block in range(quads // groups):
        buf = block % 2
        for s in range(subs):
            cols = pl.ds(s * face, face)
            cond = cond_ref[s]
            group = lax.shift_right_logical(dest_ref[:, cols], 8).astype(BF16) - block * groups
            group_all = jnp.broadcast_to(group, (vecs, face))
            for a in range(groups):
                lhs_ref[buf, a * vecs:(a + 1) * vecs, cols] = jnp.where(
                    group_all == a, cond, jnp.zeros_like(cond)
                )
        acc = dot_nt(lhs_ref[buf], hot_ref[...])
        for h in range(2):
            lanes = slice(h * 128, (h + 1) * 128)
            for a in range(groups):
                first = acc[a * vecs:a * vecs + kh, lanes].astype(BF16)
                second = turn(acc[a * vecs + kh:(a + 1) * vecs, lanes].astype(BF16))
                p = 4 * (block * groups + a) + 2 * h
                out_ref[p * tall:p * tall + kh, :] = jnp.where(mask, first, second)
                out_ref[(p + 1) * tall:(p + 1) * tall + kh, :] = jnp.where(mask, second, first)
                q = block * groups + a
                for i in range(2):
                    value = place_ref[q + i * quads:q + i * quads + 1, lanes]
                    at = (p + i) * tall + kh
                    out_ref[at:at + 2, :] = jnp.broadcast_to(value, (2, 128)).astype(BF16)
        span = pl.ds(block * 4 * groups * tall, 4 * groups * tall)
        store = pltpu.make_async_copy(out_ref.at[span], out_hbm.at[span], out_sem.at[block])
        store.start()
        stores.append(store)
    keep.wait()
    for store in stores:
        store.wait()


def local_kernel(cond_ref, schur_hbm, local_ref, schur_ref, sem):
    subs = cond_ref.shape[0]
    loads = [pltpu.make_async_copy(schur_hbm.at[s], schur_ref.at[s], sem.at[s]) for s in range(subs)]
    for copy in loads:
        copy.start()
    for s in range(subs):
        loads[s].wait()
        local_ref[s] = dot_nt(cond_ref[s], schur_ref[s])


def middle_kernel(recv_ref, inv_ref, out_ref, lhs_ref, hot_ref, high_ref):
    senders, kh = out_ref.shape[:2]
    tall = kh + 2
    vecs = 2 * kh
    blocks = inv_ref.shape[0]
    mask = low_half(kh)
    zero = jnp.zeros((kh, 128), BF16)
    for j in range(senders // 2):
        cols = pl.ds(j * 128, 128)
        at, then = 2 * j * tall, (2 * j + 1) * tall
        first = recv_ref[at:at + kh, :]
        second = recv_ref[then:then + kh, :]
        data = (jnp.where(mask, first, turn(second)), jnp.where(mask, turn(first), second))
        first = recv_ref[at + kh:at + tall, :]
        second = recv_ref[then + kh:then + tall, :]
        hot_ref[:, cols] = one_hot(128, jnp.where(mask[:2], turn(first), second)[0:1])
        high = jnp.broadcast_to(jnp.where(mask[:2], first, turn(second))[0:1], (kh, 128))
        high_ref[:, cols] = high
        for c in range(blocks):
            here = high == c
            for i in range(2):
                at = c * vecs + i * kh
                lhs_ref[at:at + kh, cols] = jnp.where(here, data[i], zero)
    summed = dot_nt(lhs_ref[...], hot_ref[...]).astype(BF16)
    solved = jnp.concatenate(
        [dot_nt(summed[c * vecs:(c + 1) * vecs], inv_ref[c]) for c in range(blocks)], axis=0
    ).astype(BF16)
    chunk = 1024
    for n in range(senders * CAP // chunk):
        found = dot_nn(solved, hot_ref[:, pl.ds(n * chunk, chunk)])
        for i in range(chunk // 128):
            lanes = slice(i * 128, (i + 1) * 128)
            j = n * (chunk // 128) + i
            high = high_ref[:, pl.ds(j * 128, 128)]
            parts = []
            for t in range(2):
                part = zero
                for c in range(blocks):
                    at = c * vecs + t * kh
                    part = jnp.where(high == c, found[at:at + kh, lanes].astype(BF16), part)
                parts.append(part)
            out_ref[2 * j] = jnp.where(mask, parts[0], turn(parts[1]))
            out_ref[2 * j + 1] = jnp.where(mask, turn(parts[0]), parts[1])


def back_kernel(
    live_ref, ret_ref, dest_ref, ires_ref, local_hbm, inv_hbm, cpl_hbm,
    inner_hbm, face_hbm,
    local_ref, inv_ref, cpl_ref, lhs_ref, hot_ref, inner_ref, face_ref, sem, out_sem,
):
    subs, vecs, inner = ires_ref.shape
    face = face_ref.shape[2]
    kh = vecs // 2
    loads = [
        pltpu.make_async_copy(local_hbm, local_ref, sem.at[0]),
        pltpu.make_async_copy(cpl_hbm, cpl_ref, sem.at[1]),
        pltpu.make_async_copy(inv_hbm, inv_ref, sem.at[2]),
    ]
    stores = [
        pltpu.make_async_copy(face_ref, face_hbm, out_sem.at[0]),
        pltpu.make_async_copy(inner_ref, inner_hbm, out_sem.at[1]),
    ]
    for copy in loads:
        copy.start()
    senders = ret_ref.shape[0]
    wide = lhs_ref.shape[1]
    groups = lhs_ref.shape[0] // vecs
    pairs = wide // 128
    mask = low_half(kh)
    for j in range(senders // 2):
        first = ret_ref[2 * j]
        second = ret_ref[2 * j + 1]
        a, i = j // pairs, j % pairs
        lanes = slice(i * 128, (i + 1) * 128)
        lhs_ref[a * vecs:a * vecs + kh, lanes] = jnp.where(mask, first, second)
        lhs_ref[a * vecs + kh:(a + 1) * vecs, lanes] = turn(jnp.where(mask, second, first))
    loads[0].wait()
    shift = wide.bit_length() - 1
    for s in range(subs):
        cols = pl.ds(s * face, face)
        dest = dest_ref[:, cols]
        within = jnp.bitwise_and(dest, wide - 1)
        for g in range(wide // 256):
            hot_ref[s, pl.ds(g * 256, 256), :] = one_hot(256, within - 256 * g)
        found = dot_nn(lhs_ref[...], hot_ref[s])
        group_all = jnp.broadcast_to(lax.shift_right_logical(dest, shift), (vecs, face))
        correction = jnp.zeros((vecs, face), F32)
        for a in range(groups):
            correction = jnp.where(group_all == a, found[a * vecs:(a + 1) * vecs], correction)
        alive = lax.broadcasted_iota(jnp.int32, (vecs, face), 1) < live_ref[s]
        face_ref[s] = jnp.where(alive, local_ref[s] + correction, 0.0).astype(BF16)
    stores[0].start()
    for copy in loads[1:]:
        copy.wait()
    extended = [
        (ires_ref[s].astype(F32) - dot_nn(face_ref[s], cpl_ref[s])).astype(BF16) for s in range(subs)
    ]
    for s in range(subs):
        inner_ref[s] = dot_nt(extended[s], inv_ref[s]).astype(BF16)
    stores[1].start()
    for copy in stores:
        copy.wait()


def vmem(count):
    return [pl.BlockSpec(memory_space=VMEM)] * count


HBM = pl.BlockSpec(memory_space=pltpu.HBM)
SMEM = pl.BlockSpec(memory_space=pltpu.SMEM)


def on_device(
    interior_res,
    interface_res,
    interior_inv,
    coupling,
    schur_inv,
    coarse_inv,
    coarse_part,
    coarse_slot,
    live_count,
):
    subs, vecs, inner = interior_res.shape
    face = interface_res.shape[2]
    rows = subs * face
    sections = lax.axis_size("sub") * lax.axis_size("grp")
    kh = vecs // 2
    groups = sections // 4
    shape = jax.ShapeDtypeStruct

    condensed, outgoing, dest = pl.pallas_call(
        front_kernel,
        name="front",
        out_shape=(
            shape((subs, vecs, face), BF16),
            shape((sections * (kh + 2), 128), BF16),
            shape((1, rows), jnp.int32),
        ),
        in_specs=[SMEM] + vmem(2) + [HBM] * 4,
        out_specs=(HBM, HBM, vmem(1)[0]),
        scratch_shapes=[
            VMEM((subs, vecs, inner), BF16),
            VMEM((subs, vecs, face), BF16),
            VMEM((subs, inner, inner), BF16),
            VMEM((subs, face, inner), BF16),
            VMEM((rows // 256 * sections, 512), BF16),
            VMEM((rows // 256 * sections, 256), BF16),
            VMEM((subs, vecs, face), BF16),
            VMEM((2, 8 * vecs, rows), BF16),
            VMEM((256, rows), BF16),
            VMEM((sections // 2, rows), BF16),
            VMEM((sections // 2, 256), F32),
            VMEM((sections * (kh + 2), 128), BF16),
            pltpu.SemaphoreType.DMA((2, subs)),
            pltpu.SemaphoreType.DMA((2,)),
            pltpu.SemaphoreType.DMA((sections // 32,)),
            pltpu.SemaphoreType.DMA(()),
        ],
        cost_estimate=pl.CostEstimate(flops=3 * 10**9, bytes_accessed=5 * 10**6, transcendentals=0),
    )(
        live_count, coarse_part.reshape(1, rows), coarse_slot.reshape(1, rows),
        interior_res, interface_res, interior_inv, coupling,
    )

    paired = outgoing.reshape(sections * (kh + 2) // 2, 2, 128)
    received = lax.all_to_all(paired, AXES, split_axis=0, concat_axis=0, tiled=True)
    received = received.reshape(sections * (kh + 2), 128)

    local = pl.pallas_call(
        local_kernel,
        name="local",
        compiler_params=pltpu.CompilerParams(vmem_limit_bytes=56 * 2**20),
        out_shape=shape((subs, vecs, face), F32),
        in_specs=vmem(1) + [HBM],
        out_specs=vmem(1)[0],
        scratch_shapes=[VMEM((subs, face, face), BF16), pltpu.SemaphoreType.DMA((subs,))],
        cost_estimate=pl.CostEstimate(
            flops=2 * rows * vecs * face, bytes_accessed=5 * 10**6, transcendentals=0
        ),
    )(condensed, schur_inv)

    blocks = coarse_inv.shape[0] // lax.axis_size("sub")
    mine = lax.dynamic_slice_in_dim(coarse_inv, lax.axis_index("sub") * blocks, blocks, 0)
    replies = pl.pallas_call(
        middle_kernel,
        name="middle",
        compiler_params=pltpu.CompilerParams(vmem_limit_bytes=24 * 2**20),
        out_shape=shape((sections, kh, 128), BF16),
        in_specs=vmem(2),
        out_specs=vmem(1)[0],
        scratch_shapes=[
            VMEM((blocks * vecs, sections * CAP), BF16),
            VMEM((128, sections * CAP), BF16),
            VMEM((kh, sections * CAP), BF16),
        ],
        cost_estimate=pl.CostEstimate(flops=10**9, bytes_accessed=2 * 10**6, transcendentals=0),
    )(received, mine)

    returned = lax.all_to_all(replies, AXES, split_axis=0, concat_axis=0, tiled=True)

    return pl.pallas_call(
        back_kernel,
        name="back",
        compiler_params=pltpu.CompilerParams(vmem_limit_bytes=53 * 2**20),
        out_shape=(shape((subs, vecs, inner), BF16), shape((subs, vecs, face), BF16)),
        in_specs=[SMEM] + vmem(3) + [HBM] * 3,
        out_specs=(HBM, HBM),
        scratch_shapes=[
            VMEM((subs, vecs, face), F32),
            VMEM((subs, inner, inner), BF16),
            VMEM((subs, face, inner), BF16),
            VMEM((16 * vecs, sections * CAP // 16), BF16),
            VMEM((subs, sections * CAP // 16, face), BF16),
            VMEM((subs, vecs, inner), BF16),
            VMEM((subs, vecs, face), BF16),
            pltpu.SemaphoreType.DMA((3,)),
            pltpu.SemaphoreType.DMA((2,)),
        ],
        cost_estimate=pl.CostEstimate(flops=3 * 10**9, bytes_accessed=6 * 10**6, transcendentals=0),
    )(live_count, returned, dest, interior_res, local, interior_inv, coupling)


def solution(mesh):
    rows = P(AXES)
    in_specs = (rows, rows, rows, rows, rows, P("grp"), rows, rows, rows)
    return jax.shard_map(
        on_device, mesh=mesh, in_specs=in_specs, out_specs=(rows, rows), check_vma=False
    )
```

```python
import jax
import jax.numpy as jnp
from jax import lax
from jax.experimental import pallas as pl
from jax.experimental.pallas import tpu as pltpu
from jax.sharding import PartitionSpec as P

F32 = jnp.float32
BF16 = jnp.bfloat16
AXES = ("sub", "grp")
CAP = 64
VMEM = pltpu.VMEM
HALF = 64


def dot_nn(left, right):
    return lax.dot_general(left, right, (((1,), (0,)), ((), ())), preferred_element_type=F32)


def dot_nt(left, right):
    return lax.dot_general(left, right, (((1,), (1,)), ((), ())), preferred_element_type=F32)


def low_half(rows):
    return lax.broadcasted_iota(jnp.int32, (rows, 128), 1).astype(BF16) < HALF


def turn(tile):
    return jnp.concatenate([tile[:, HALF:], tile[:, :HALF]], axis=1)


def swap_pair(first, second):
    mask = lax.broadcasted_iota(jnp.int32, first.shape, 1) < HALF
    even = jnp.where(mask, first, pltpu.roll(second, HALF, 1))
    odd = jnp.where(mask, pltpu.roll(first, HALF, 1), second)
    return even, odd


def one_hot(count, index):
    shape = (count, index.shape[1])
    rows = lax.broadcasted_iota(jnp.int32, shape, 0).astype(BF16)
    wanted = jnp.broadcast_to(index.astype(BF16), shape)
    return jnp.where(rows == wanted, jnp.ones(shape, BF16), jnp.zeros(shape, BF16))


def front_kernel(
    live_ref, part_ref, slot_ref, ires_hbm, fres_hbm, inv_hbm, cpl_hbm,
    cond_hbm, out_hbm, dest_hbm,
    ires_ref, fres_ref, inv_ref, cpl_ref, mark_ref, own_ref, cond_ref, lhs_ref, hot_ref, mark_slot_ref, place_ref, out_ref, dest_ref,
    sem, res_sem, out_sem, keep_sem,
):
    subs, vecs, inner = ires_ref.shape
    face = fres_ref.shape[2]
    residuals = [
        pltpu.make_async_copy(ires_hbm, ires_ref, res_sem.at[0]),
        pltpu.make_async_copy(fres_hbm, fres_ref, res_sem.at[1]),
    ]
    loads = []
    for copy in residuals:
        copy.start()
    for s in range(subs):
        one = pltpu.make_async_copy(inv_hbm.at[s], inv_ref.at[s], sem.at[0, s])
        two = pltpu.make_async_copy(cpl_hbm.at[s], cpl_ref.at[s], sem.at[1, s])
        loads.append((one, two))
    for i in range(2):
        for s in range(subs):
            loads[s][i].start()

    width = 256
    tall = vecs // 2 + 2
    sections = out_ref.shape[0] // tall
    chunks = subs * face // width
    row = lax.broadcasted_iota(jnp.int32, (width, width), 0)
    column = lax.broadcasted_iota(jnp.int32, (width, width), 1)
    counter = jnp.where(row <= column, 1.0, 0.0).astype(BF16)
    for c in range(chunks):
        mark_ref[pl.ds(c * sections, sections), :] = one_hot(sections, part_ref[:, pl.ds(c * width, width)])
    counted = dot_nn(mark_ref[...], counter)
    run = jnp.zeros((sections, width), F32)
    for c in range(chunks):
        block = slice(c * sections, (c + 1) * sections)
        within = counted[block]
        total = (within + run).astype(BF16)
        own_ref[block, :] = jnp.where(mark_ref[block, :] > 0, total, jnp.zeros_like(total))
        run = run + jnp.broadcast_to(within[:, width - 1:width], (sections, width))
    chunk_row = lax.broadcasted_iota(jnp.int32, (chunks, chunks * sections), 0)
    chunk_of = lax.broadcasted_iota(jnp.int32, (chunks, chunks * sections), 1) // sections
    place = dot_nn(jnp.where(chunk_row == chunk_of, 1.0, 0.0).astype(BF16), own_ref[...])
    place = place.astype(jnp.int32) - 1
    for c in range(chunks):
        cols = pl.ds(c * width, width)
        dest_ref[:, cols] = part_ref[:, cols] * CAP + place[c:c + 1]
    quads = sections // 4

    @pl.when(live_ref[0] >= 0)
    def _():
        for copy in residuals:
            copy.wait()
        for s in range(subs):
            loads[s][0].wait()
        for s in range(subs):
            loads[s][1].wait()
        for s in range(subs):
            cols = pl.ds(s * face, face)
            dest = dest_ref[:, cols]
            hot_ref[:, cols] = one_hot(256, jnp.bitwise_and(dest, 255))
            mine = one_hot(quads, lax.shift_right_logical(dest, 8))
            slot = slot_ref[:, cols]
            high = lax.shift_right_logical(slot, 7).astype(BF16)
            low = jnp.bitwise_and(slot, 127).astype(BF16)
            mark_slot_ref[0:quads, cols] = mine * jnp.broadcast_to(high, mine.shape)
            mark_slot_ref[quads:2 * quads, cols] = mine * jnp.broadcast_to(low, mine.shape)
        slots = dot_nt(mark_slot_ref[...], hot_ref[...])
        for h in range(2):
            lanes = slice(h * 128, (h + 1) * 128)
            even, odd = swap_pair(slots[0:quads, lanes], slots[quads:2 * quads, lanes])
            place_ref[0:quads, lanes] = even
            place_ref[quads:2 * quads, lanes] = odd
        pres = [dot_nt(ires_ref[s], inv_ref[s]).astype(BF16) for s in range(subs)]
        for s in range(subs):
            cond = fres_ref[s].astype(F32) - dot_nt(pres[s], cpl_ref[s])
            alive = lax.broadcasted_iota(jnp.int32, (vecs, face), 1) < live_ref[s]
            cond_ref[s] = jnp.where(alive, cond, 0.0).astype(BF16)
    keeps = [
        pltpu.make_async_copy(cond_ref, cond_hbm, keep_sem.at[0]),
        pltpu.make_async_copy(dest_ref, dest_hbm, keep_sem.at[1]),
    ]
    for copy in keeps:
        copy.start()

    groups = 8
    kh = vecs // 2
    mask = low_half(kh)
    stores = []
    for block in range(quads // groups):
        buf = block % 2
        for s in range(subs):
            cols = pl.ds(s * face, face)
            cond = cond_ref[s]
            group = lax.shift_right_logical(dest_ref[:, cols], 8).astype(BF16) - block * groups
            group_all = jnp.broadcast_to(group, (vecs, face))
            for a in range(groups):
                lhs_ref[buf, a * vecs:(a + 1) * vecs, cols] = jnp.where(
                    group_all == a, cond, jnp.zeros_like(cond)
                )
        acc = dot_nt(lhs_ref[buf], hot_ref[...])
        for h in range(2):
            lanes = slice(h * 128, (h + 1) * 128)
            for a in range(groups):
                first = acc[a * vecs:a * vecs + kh, lanes].astype(BF16)
                second = turn(acc[a * vecs + kh:(a + 1) * vecs, lanes].astype(BF16))
                p = 4 * (block * groups + a) + 2 * h
                out_ref[p * tall:p * tall + kh, :] = jnp.where(mask, first, second)
                out_ref[(p + 1) * tall:(p + 1) * tall + kh, :] = jnp.where(mask, second, first)
                q = block * groups + a
                for i in range(2):
                    value = place_ref[q + i * quads:q + i * quads + 1, lanes]
                    at = (p + i) * tall + kh
                    out_ref[at:at + 2, :] = jnp.broadcast_to(value, (2, 128)).astype(BF16)
        span = pl.ds(block * 4 * groups * tall, 4 * groups * tall)
        store = pltpu.make_async_copy(out_ref.at[span], out_hbm.at[span], out_sem.at[block])
        store.start()
        stores.append(store)
    for copy in keeps + stores:
        copy.wait()


def local_kernel(cond_ref, schur_hbm, local_ref, schur_ref, sem):
    subs = cond_ref.shape[0]
    loads = [pltpu.make_async_copy(schur_hbm.at[s], schur_ref.at[s], sem.at[s]) for s in range(subs)]
    for copy in loads:
        copy.start()
    for s in range(subs):
        loads[s].wait()
        local_ref[s] = dot_nt(cond_ref[s], schur_ref[s])


def middle_kernel(recv_ref, inv_ref, out_hbm, lhs_ref, hot_ref, high_ref, out_ref, sem):
    senders, kh = out_ref.shape[:2]
    tall = kh + 2
    vecs = 2 * kh
    blocks = inv_ref.shape[0]
    mask = low_half(kh)
    zero = jnp.zeros((kh, 128), BF16)
    for j in range(senders // 2):
        cols = pl.ds(j * 128, 128)
        at, then = 2 * j * tall, (2 * j + 1) * tall
        first = recv_ref[at:at + kh, :]
        second = recv_ref[then:then + kh, :]
        data = (jnp.where(mask, first, turn(second)), jnp.where(mask, turn(first), second))
        first = recv_ref[at + kh:at + tall, :]
        second = recv_ref[then + kh:then + tall, :]
        hot_ref[:, cols] = one_hot(128, jnp.where(mask[:2], turn(first), second)[0:1])
        high = jnp.broadcast_to(jnp.where(mask[:2], first, turn(second))[0:1], (kh, 128))
        high_ref[:, cols] = high
        for c in range(blocks):
            here = high == c
            for i in range(2):
                at = c * vecs + i * kh
                lhs_ref[at:at + kh, cols] = jnp.where(here, data[i], zero)
    summed = dot_nt(lhs_ref[...], hot_ref[...]).astype(BF16)
    solved = jnp.concatenate(
        [dot_nt(summed[c * vecs:(c + 1) * vecs], inv_ref[c]) for c in range(blocks)], axis=0
    ).astype(BF16)
    chunk = 1024
    stores = []
    for n in range(senders * CAP // chunk):
        found = dot_nn(solved, hot_ref[:, pl.ds(n * chunk, chunk)])
        for i in range(chunk // 128):
            lanes = slice(i * 128, (i + 1) * 128)
            j = n * (chunk // 128) + i
            high = high_ref[:, pl.ds(j * 128, 128)]
            parts = []
            for t in range(2):
                part = zero
                for c in range(blocks):
                    at = c * vecs + t * kh
                    part = jnp.where(high == c, found[at:at + kh, lanes].astype(BF16), part)
                parts.append(part)
            out_ref[2 * j] = jnp.where(mask, parts[0], turn(parts[1]))
            out_ref[2 * j + 1] = jnp.where(mask, turn(parts[0]), parts[1])
        span = pl.ds(n * (chunk // CAP), chunk // CAP)
        store = pltpu.make_async_copy(out_ref.at[span], out_hbm.at[span], sem.at[n])
        store.start()
        stores.append(store)
    for store in stores:
        store.wait()


def back_kernel(
    live_ref, ret_ref, dest_ref, ires_ref, local_hbm, inv_hbm, cpl_hbm,
    inner_hbm, face_hbm,
    local_ref, inv_ref, cpl_ref, lhs_ref, hot_ref, inner_ref, face_ref, sem, out_sem,
):
    subs, vecs, inner = ires_ref.shape
    face = face_ref.shape[2]
    kh = vecs // 2
    loads = [
        pltpu.make_async_copy(local_hbm, local_ref, sem.at[0]),
        pltpu.make_async_copy(cpl_hbm, cpl_ref, sem.at[1]),
        pltpu.make_async_copy(inv_hbm, inv_ref, sem.at[2]),
    ]
    stores = [
        pltpu.make_async_copy(face_ref, face_hbm, out_sem.at[0]),
        pltpu.make_async_copy(inner_ref, inner_hbm, out_sem.at[1]),
    ]
    for copy in loads:
        copy.start()
    senders = ret_ref.shape[0]
    wide = lhs_ref.shape[1]
    groups = lhs_ref.shape[0] // vecs
    pairs = wide // 128
    mask = low_half(kh)
    for j in range(senders // 2):
        first = ret_ref[2 * j]
        second = ret_ref[2 * j + 1]
        a, i = j // pairs, j % pairs
        lanes = slice(i * 128, (i + 1) * 128)
        lhs_ref[a * vecs:a * vecs + kh, lanes] = jnp.where(mask, first, second)
        lhs_ref[a * vecs + kh:(a + 1) * vecs, lanes] = turn(jnp.where(mask, second, first))
    loads[0].wait()
    shift = wide.bit_length() - 1
    for s in range(subs):
        cols = pl.ds(s * face, face)
        dest = dest_ref[:, cols]
        within = jnp.bitwise_and(dest, wide - 1)
        for g in range(wide // 256):
            hot_ref[s, pl.ds(g * 256, 256), :] = one_hot(256, within - 256 * g)
        found = dot_nn(lhs_ref[...], hot_ref[s])
        group_all = jnp.broadcast_to(lax.shift_right_logical(dest, shift), (vecs, face))
        correction = jnp.zeros((vecs, face), F32)
        for a in range(groups):
            correction = jnp.where(group_all == a, found[a * vecs:(a + 1) * vecs], correction)
        alive = lax.broadcasted_iota(jnp.int32, (vecs, face), 1) < live_ref[s]
        face_ref[s] = jnp.where(alive, local_ref[s] + correction, 0.0).astype(BF16)
    stores[0].start()
    for copy in loads[1:]:
        copy.wait()
    extended = [
        (ires_ref[s].astype(F32) - dot_nn(face_ref[s], cpl_ref[s])).astype(BF16) for s in range(subs)
    ]
    for s in range(subs):
        inner_ref[s] = dot_nt(extended[s], inv_ref[s]).astype(BF16)
    stores[1].start()
    for copy in stores:
        copy.wait()


def vmem(count):
    return [pl.BlockSpec(memory_space=VMEM)] * count


HBM = pl.BlockSpec(memory_space=pltpu.HBM)
SMEM = pl.BlockSpec(memory_space=pltpu.SMEM)


def on_device(
    interior_res,
    interface_res,
    interior_inv,
    coupling,
    schur_inv,
    coarse_inv,
    coarse_part,
    coarse_slot,
    live_count,
):
    subs, vecs, inner = interior_res.shape
    face = interface_res.shape[2]
    rows = subs * face
    sections = lax.axis_size("sub") * lax.axis_size("grp")
    kh = vecs // 2
    groups = sections // 4
    shape = jax.ShapeDtypeStruct

    condensed, outgoing, dest = pl.pallas_call(
        front_kernel,
        name="front",
        out_shape=(
            shape((subs, vecs, face), BF16),
            shape((sections * (kh + 2), 128), BF16),
            shape((1, rows), jnp.int32),
        ),
        in_specs=[SMEM] + vmem(2) + [HBM] * 4,
        out_specs=(HBM, HBM, HBM),
        scratch_shapes=[
            VMEM((subs, vecs, inner), BF16),
            VMEM((subs, vecs, face), BF16),
            VMEM((subs, inner, inner), BF16),
            VMEM((subs, face, inner), BF16),
            VMEM((rows // 256 * sections, 256), BF16),
            VMEM((rows // 256 * sections, 256), BF16),
            VMEM((subs, vecs, face), BF16),
            VMEM((2, 8 * vecs, rows), BF16),
            VMEM((256, rows), BF16),
            VMEM((sections // 2, rows), BF16),
            VMEM((sections // 2, 256), F32),
            VMEM((sections * (kh + 2), 128), BF16),
            VMEM((1, rows), jnp.int32),
            pltpu.SemaphoreType.DMA((2, subs)),
            pltpu.SemaphoreType.DMA((2,)),
            pltpu.SemaphoreType.DMA((sections // 32,)),
            pltpu.SemaphoreType.DMA((2,)),
        ],
        cost_estimate=pl.CostEstimate(flops=3 * 10**9, bytes_accessed=5 * 10**6, transcendentals=0),
    )(
        live_count, coarse_part.reshape(1, rows), coarse_slot.reshape(1, rows),
        interior_res, interface_res, interior_inv, coupling,
    )

    paired = outgoing.reshape(sections * (kh + 2) // 2, 2, 128)
    received = lax.all_to_all(paired, AXES, split_axis=0, concat_axis=0, tiled=True)
    received = received.reshape(sections * (kh + 2), 128)

    local = pl.pallas_call(
        local_kernel,
        name="local",
        compiler_params=pltpu.CompilerParams(vmem_limit_bytes=56 * 2**20),
        out_shape=shape((subs, vecs, face), F32),
        in_specs=vmem(1) + [HBM],
        out_specs=vmem(1)[0],
        scratch_shapes=[VMEM((subs, face, face), BF16), pltpu.SemaphoreType.DMA((subs,))],
        cost_estimate=pl.CostEstimate(
            flops=2 * rows * vecs * face, bytes_accessed=5 * 10**6, transcendentals=0
        ),
    )(condensed, schur_inv)

    blocks = coarse_inv.shape[0] // lax.axis_size("sub")
    mine = lax.dynamic_slice_in_dim(coarse_inv, lax.axis_index("sub") * blocks, blocks, 0)
    replies = pl.pallas_call(
        middle_kernel,
        name="middle",
        compiler_params=pltpu.CompilerParams(vmem_limit_bytes=24 * 2**20),
        out_shape=shape((sections, kh, 128), BF16),
        in_specs=vmem(2),
        out_specs=HBM,
        scratch_shapes=[
            VMEM((blocks * vecs, sections * CAP), BF16),
            VMEM((128, sections * CAP), BF16),
            VMEM((kh, sections * CAP), BF16),
            VMEM((sections, kh, 128), BF16),
            pltpu.SemaphoreType.DMA((sections * CAP // 1024,)),
        ],
        cost_estimate=pl.CostEstimate(flops=10**9, bytes_accessed=2 * 10**6, transcendentals=0),
    )(received, mine)

    returned = lax.all_to_all(replies, AXES, split_axis=0, concat_axis=0, tiled=True)

    return pl.pallas_call(
        back_kernel,
        name="back",
        compiler_params=pltpu.CompilerParams(vmem_limit_bytes=53 * 2**20),
        out_shape=(shape((subs, vecs, inner), BF16), shape((subs, vecs, face), BF16)),
        in_specs=[SMEM] + vmem(3) + [HBM] * 3,
        out_specs=(HBM, HBM),
        scratch_shapes=[
            VMEM((subs, vecs, face), F32),
            VMEM((subs, inner, inner), BF16),
            VMEM((subs, face, inner), BF16),
            VMEM((16 * vecs, sections * CAP // 16), BF16),
            VMEM((subs, sections * CAP // 16, face), BF16),
            VMEM((subs, vecs, inner), BF16),
            VMEM((subs, vecs, face), BF16),
            pltpu.SemaphoreType.DMA((3,)),
            pltpu.SemaphoreType.DMA((2,)),
        ],
        cost_estimate=pl.CostEstimate(flops=3 * 10**9, bytes_accessed=6 * 10**6, transcendentals=0),
    )(live_count, returned, dest, interior_res, local, interior_inv, coupling)


def solution(mesh):
    rows = P(AXES)
    in_specs = (rows, rows, rows, rows, rows, P("grp"), rows, rows, rows)
    return jax.shard_map(
        on_device, mesh=mesh, in_specs=in_specs, out_specs=(rows, rows), check_vma=False
    )
```

```python
import jax
import jax.numpy as jnp
from jax import lax
from jax.experimental import pallas as pl
from jax.experimental.pallas import tpu as pltpu
from jax.sharding import PartitionSpec as P

F32 = jnp.float32
BF16 = jnp.bfloat16
AXES = ("sub", "grp")
CAP = 64
VMEM = pltpu.VMEM
HALF = 64


def dot_nn(left, right):
    return lax.dot_general(left, right, (((1,), (0,)), ((), ())), preferred_element_type=F32)


def dot_nt(left, right):
    return lax.dot_general(left, right, (((1,), (1,)), ((), ())), preferred_element_type=F32)


def low_half(rows):
    return lax.broadcasted_iota(jnp.int32, (rows, 128), 1).astype(BF16) < HALF


def turn(tile):
    return jnp.concatenate([tile[:, HALF:], tile[:, :HALF]], axis=1)


def swap_pair(first, second):
    mask = lax.broadcasted_iota(jnp.int32, first.shape, 1) < HALF
    even = jnp.where(mask, first, pltpu.roll(second, HALF, 1))
    odd = jnp.where(mask, pltpu.roll(first, HALF, 1), second)
    return even, odd


def one_hot(count, index):
    shape = (count, index.shape[1])
    rows = lax.broadcasted_iota(jnp.int32, shape, 0).astype(BF16)
    wanted = jnp.broadcast_to(index.astype(BF16), shape)
    return jnp.where(rows == wanted, jnp.ones(shape, BF16), jnp.zeros(shape, BF16))


def front_kernel(
    live_ref, part_ref, slot_ref, ires_hbm, fres_hbm, inv_hbm, cpl_hbm,
    cond_hbm, out_hbm, dest_hbm,
    ires_ref, fres_ref, inv_ref, cpl_ref, mark_ref, own_ref, cond_ref, lhs_ref, hot_ref, mark_slot_ref, place_ref, out_ref, dest_ref,
    sem, res_sem, out_sem, keep_sem,
):
    subs, vecs, inner = ires_ref.shape
    face = fres_ref.shape[2]
    residuals = [
        pltpu.make_async_copy(ires_hbm, ires_ref, res_sem.at[0]),
        pltpu.make_async_copy(fres_hbm, fres_ref, res_sem.at[1]),
    ]
    loads = []
    for copy in residuals:
        copy.start()
    for s in range(subs):
        one = pltpu.make_async_copy(inv_hbm.at[s], inv_ref.at[s], sem.at[0, s])
        two = pltpu.make_async_copy(cpl_hbm.at[s], cpl_ref.at[s], sem.at[1, s])
        loads.append((one, two))
    for i in range(2):
        for s in range(subs):
            loads[s][i].start()

    width = 256
    tall = vecs // 2 + 2
    sections = out_ref.shape[0] // tall
    chunks = subs * face // width
    row = lax.broadcasted_iota(jnp.int32, (width, width), 0)
    column = lax.broadcasted_iota(jnp.int32, (width, width), 1)
    counter = jnp.where(row <= column, 1.0, 0.0).astype(BF16)
    for c in range(chunks):
        mark_ref[pl.ds(c * sections, sections), :] = one_hot(sections, part_ref[:, pl.ds(c * width, width)])
    counted = dot_nn(mark_ref[...], counter)
    run = jnp.zeros((sections, width), F32)
    for c in range(chunks):
        block = slice(c * sections, (c + 1) * sections)
        within = counted[block]
        total = (within + run).astype(BF16)
        own_ref[block, :] = jnp.where(mark_ref[block, :] > 0, total, jnp.zeros_like(total))
        run = run + jnp.broadcast_to(within[:, width - 1:width], (sections, width))
    chunk_row = lax.broadcasted_iota(jnp.int32, (chunks, chunks * sections), 0)
    chunk_of = lax.broadcasted_iota(jnp.int32, (chunks, chunks * sections), 1) // sections
    place = dot_nn(jnp.where(chunk_row == chunk_of, 1.0, 0.0).astype(BF16), own_ref[...])
    place = place.astype(jnp.int32) - 1
    for c in range(chunks):
        cols = pl.ds(c * width, width)
        dest_ref[:, cols] = part_ref[:, cols] * CAP + place[c:c + 1]
    quads = sections // 4

    @pl.when(live_ref[0] >= 0)
    def _():
        for copy in residuals:
            copy.wait()
        for s in range(subs):
            loads[s][0].wait()
        for s in range(subs):
            loads[s][1].wait()
        for s in range(subs):
            cols = pl.ds(s * face, face)
            dest = dest_ref[:, cols]
            hot_ref[:, cols] = one_hot(256, jnp.bitwise_and(dest, 255))
            mine = one_hot(quads, lax.shift_right_logical(dest, 8))
            slot = slot_ref[:, cols]
            high = lax.shift_right_logical(slot, 7).astype(BF16)
            low = jnp.bitwise_and(slot, 127).astype(BF16)
            mark_slot_ref[0:quads, cols] = mine * jnp.broadcast_to(high, mine.shape)
            mark_slot_ref[quads:2 * quads, cols] = mine * jnp.broadcast_to(low, mine.shape)
        slots = dot_nt(mark_slot_ref[...], hot_ref[...])
        for h in range(2):
            lanes = slice(h * 128, (h + 1) * 128)
            even, odd = swap_pair(slots[0:quads, lanes], slots[quads:2 * quads, lanes])
            place_ref[0:quads, lanes] = even
            place_ref[quads:2 * quads, lanes] = odd
        pres = [dot_nt(ires_ref[s], inv_ref[s]).astype(BF16) for s in range(subs)]
        for s in range(subs):
            cond = fres_ref[s].astype(F32) - dot_nt(pres[s], cpl_ref[s])
            alive = lax.broadcasted_iota(jnp.int32, (vecs, face), 1) < live_ref[s]
            cond_ref[s] = jnp.where(alive, cond, 0.0).astype(BF16)
    keeps = [
        pltpu.make_async_copy(cond_ref, cond_hbm, keep_sem.at[0]),
        pltpu.make_async_copy(dest_ref, dest_hbm, keep_sem.at[1]),
    ]
    for copy in keeps:
        copy.start()

    groups = 8
    kh = vecs // 2
    mask = low_half(kh)
    stores = []
    for block in range(quads // groups):
        buf = block % 2
        for s in range(subs):
            cols = pl.ds(s * face, face)
            cond = cond_ref[s]
            group = lax.shift_right_logical(dest_ref[:, cols], 8).astype(BF16) - block * groups
            group_all = jnp.broadcast_to(group, (vecs, face))
            for a in range(groups):
                lhs_ref[buf, a * vecs:(a + 1) * vecs, cols] = jnp.where(
                    group_all == a, cond, jnp.zeros_like(cond)
                )
        acc = dot_nt(lhs_ref[buf], hot_ref[...])
        for h in range(2):
            lanes = slice(h * 128, (h + 1) * 128)
            for a in range(groups):
                first = acc[a * vecs:a * vecs + kh, lanes].astype(BF16)
                second = turn(acc[a * vecs + kh:(a + 1) * vecs, lanes].astype(BF16))
                p = 4 * (block * groups + a) + 2 * h
                out_ref[p * tall:p * tall + kh, :] = jnp.where(mask, first, second)
                out_ref[(p + 1) * tall:(p + 1) * tall + kh, :] = jnp.where(mask, second, first)
                q = block * groups + a
                for i in range(2):
                    value = place_ref[q + i * quads:q + i * quads + 1, lanes]
                    at = (p + i) * tall + kh
                    out_ref[at:at + 2, :] = jnp.broadcast_to(value, (2, 128)).astype(BF16)
        span = pl.ds(block * 4 * groups * tall, 4 * groups * tall)
        store = pltpu.make_async_copy(out_ref.at[span], out_hbm.at[span], out_sem.at[block])
        store.start()
        stores.append(store)
    for copy in keeps + stores:
        copy.wait()


def local_kernel(cond_ref, schur_hbm, local_ref, schur_ref, sem):
    subs = cond_ref.shape[0]
    loads = [pltpu.make_async_copy(schur_hbm.at[s], schur_ref.at[s], sem.at[s]) for s in range(subs)]
    for copy in loads:
        copy.start()
    for s in range(subs):
        loads[s].wait()
        local_ref[s] = dot_nt(cond_ref[s], schur_ref[s])


def middle_kernel(recv_ref, inv_ref, out_hbm, lhs_ref, hot_ref, high_ref, out_ref, sem):
    senders, kh = out_ref.shape[:2]
    tall = kh + 2
    vecs = 2 * kh
    blocks = inv_ref.shape[0]
    mask = low_half(kh)
    zero = jnp.zeros((kh, 128), BF16)
    for j in range(senders // 2):
        cols = pl.ds(j * 128, 128)
        at, then = 2 * j * tall, (2 * j + 1) * tall
        first = recv_ref[at:at + kh, :]
        second = recv_ref[then:then + kh, :]
        data = (jnp.where(mask, first, turn(second)), jnp.where(mask, turn(first), second))
        first = recv_ref[at + kh:at + tall, :]
        second = recv_ref[then + kh:then + tall, :]
        hot_ref[:, cols] = one_hot(128, jnp.where(mask[:2], turn(first), second)[0:1])
        high = jnp.broadcast_to(jnp.where(mask[:2], first, turn(second))[0:1], (kh, 128))
        high_ref[:, cols] = high
        for c in range(blocks):
            here = high == c
            for i in range(2):
                at = c * vecs + i * kh
                lhs_ref[at:at + kh, cols] = jnp.where(here, data[i], zero)
    summed = dot_nt(lhs_ref[...], hot_ref[...]).astype(BF16)
    solved = jnp.concatenate(
        [dot_nt(summed[c * vecs:(c + 1) * vecs], inv_ref[c]) for c in range(blocks)], axis=0
    ).astype(BF16)
    chunk = 1024
    stores = []
    for n in range(senders * CAP // chunk):
        found = dot_nn(solved, hot_ref[:, pl.ds(n * chunk, chunk)])
        for i in range(chunk // 128):
            lanes = slice(i * 128, (i + 1) * 128)
            j = n * (chunk // 128) + i
            high = high_ref[:, pl.ds(j * 128, 128)]
            parts = []
            for t in range(2):
                part = zero
                for c in range(blocks):
                    at = c * vecs + t * kh
                    part = jnp.where(high == c, found[at:at + kh, lanes].astype(BF16), part)
                parts.append(part)
            out_ref[2 * j] = jnp.where(mask, parts[0], turn(parts[1]))
            out_ref[2 * j + 1] = jnp.where(mask, turn(parts[0]), parts[1])
        span = pl.ds(n * (chunk // CAP), chunk // CAP)
        store = pltpu.make_async_copy(out_ref.at[span], out_hbm.at[span], sem.at[n])
        store.start()
        stores.append(store)
    for store in stores:
        store.wait()


def back_kernel(
    live_ref, ret_ref, dest_ref, ires_ref, local_hbm, inv_hbm, cpl_hbm,
    inner_hbm, face_hbm,
    local_ref, inv_ref, cpl_ref, lhs_ref, hot_ref, inner_ref, face_ref, sem, out_sem,
):
    subs, vecs, inner = ires_ref.shape
    face = face_ref.shape[2]
    kh = vecs // 2
    loads = [
        pltpu.make_async_copy(local_hbm, local_ref, sem.at[0]),
        pltpu.make_async_copy(cpl_hbm, cpl_ref, sem.at[1]),
        pltpu.make_async_copy(inv_hbm, inv_ref, sem.at[2]),
    ]
    stores = [
        pltpu.make_async_copy(inner_ref.at[s], inner_hbm.at[s], out_sem.at[s]) for s in range(subs)
    ]
    stores.append(pltpu.make_async_copy(face_ref, face_hbm, out_sem.at[subs]))
    for copy in loads:
        copy.start()
    senders = ret_ref.shape[0]
    wide = lhs_ref.shape[1]
    groups = lhs_ref.shape[0] // vecs
    pairs = wide // 128
    mask = low_half(kh)
    for j in range(senders // 2):
        first = ret_ref[2 * j]
        second = ret_ref[2 * j + 1]
        a, i = j // pairs, j % pairs
        lanes = slice(i * 128, (i + 1) * 128)
        lhs_ref[a * vecs:a * vecs + kh, lanes] = jnp.where(mask, first, second)
        lhs_ref[a * vecs + kh:(a + 1) * vecs, lanes] = turn(jnp.where(mask, second, first))
    loads[0].wait()
    shift = wide.bit_length() - 1
    for s in range(subs):
        cols = pl.ds(s * face, face)
        dest = dest_ref[:, cols]
        within = jnp.bitwise_and(dest, wide - 1)
        for g in range(wide // 256):
            hot_ref[s, pl.ds(g * 256, 256), :] = one_hot(256, within - 256 * g)
        found = dot_nn(lhs_ref[...], hot_ref[s])
        group_all = jnp.broadcast_to(lax.shift_right_logical(dest, shift), (vecs, face))
        correction = jnp.zeros((vecs, face), F32)
        for a in range(groups):
            correction = jnp.where(group_all == a, found[a * vecs:(a + 1) * vecs], correction)
        alive = lax.broadcasted_iota(jnp.int32, (vecs, face), 1) < live_ref[s]
        face_ref[s] = jnp.where(alive, local_ref[s] + correction, 0.0).astype(BF16)
    stores[subs].start()
    for copy in loads[1:]:
        copy.wait()
    extended = [
        (ires_ref[s].astype(F32) - dot_nn(face_ref[s], cpl_ref[s])).astype(BF16) for s in range(subs)
    ]
    for s in range(subs):
        inner_ref[s] = dot_nt(extended[s], inv_ref[s]).astype(BF16)
        stores[s].start()
    for copy in stores:
        copy.wait()


def vmem(count):
    return [pl.BlockSpec(memory_space=VMEM)] * count


HBM = pl.BlockSpec(memory_space=pltpu.HBM)
SMEM = pl.BlockSpec(memory_space=pltpu.SMEM)


def on_device(
    interior_res,
    interface_res,
    interior_inv,
    coupling,
    schur_inv,
    coarse_inv,
    coarse_part,
    coarse_slot,
    live_count,
):
    subs, vecs, inner = interior_res.shape
    face = interface_res.shape[2]
    rows = subs * face
    sections = lax.axis_size("sub") * lax.axis_size("grp")
    kh = vecs // 2
    groups = sections // 4
    shape = jax.ShapeDtypeStruct

    condensed, outgoing, dest = pl.pallas_call(
        front_kernel,
        name="front",
        out_shape=(
            shape((subs, vecs, face), BF16),
            shape((sections * (kh + 2), 128), BF16),
            shape((1, rows), jnp.int32),
        ),
        in_specs=[SMEM] + vmem(2) + [HBM] * 4,
        out_specs=(HBM, HBM, HBM),
        scratch_shapes=[
            VMEM((subs, vecs, inner), BF16),
            VMEM((subs, vecs, face), BF16),
            VMEM((subs, inner, inner), BF16),
            VMEM((subs, face, inner), BF16),
            VMEM((rows // 256 * sections, 256), BF16),
            VMEM((rows // 256 * sections, 256), BF16),
            VMEM((subs, vecs, face), BF16),
            VMEM((2, 8 * vecs, rows), BF16),
            VMEM((256, rows), BF16),
            VMEM((sections // 2, rows), BF16),
            VMEM((sections // 2, 256), F32),
            VMEM((sections * (kh + 2), 128), BF16),
            VMEM((1, rows), jnp.int32),
            pltpu.SemaphoreType.DMA((2, subs)),
            pltpu.SemaphoreType.DMA((2,)),
            pltpu.SemaphoreType.DMA((sections // 32,)),
            pltpu.SemaphoreType.DMA((2,)),
        ],
        cost_estimate=pl.CostEstimate(flops=3 * 10**9, bytes_accessed=5 * 10**6, transcendentals=0),
    )(
        live_count, coarse_part.reshape(1, rows), coarse_slot.reshape(1, rows),
        interior_res, interface_res, interior_inv, coupling,
    )

    paired = outgoing.reshape(sections * (kh + 2) // 2, 2, 128)
    received = lax.all_to_all(paired, AXES, split_axis=0, concat_axis=0, tiled=True)
    received = received.reshape(sections * (kh + 2), 128)

    local = pl.pallas_call(
        local_kernel,
        name="local",
        compiler_params=pltpu.CompilerParams(vmem_limit_bytes=56 * 2**20),
        out_shape=shape((subs, vecs, face), F32),
        in_specs=vmem(1) + [HBM],
        out_specs=vmem(1)[0],
        scratch_shapes=[VMEM((subs, face, face), BF16), pltpu.SemaphoreType.DMA((subs,))],
        cost_estimate=pl.CostEstimate(
            flops=2 * rows * vecs * face, bytes_accessed=5 * 10**6, transcendentals=0
        ),
    )(condensed, schur_inv)

    blocks = coarse_inv.shape[0] // lax.axis_size("sub")
    mine = lax.dynamic_slice_in_dim(coarse_inv, lax.axis_index("sub") * blocks, blocks, 0)
    replies = pl.pallas_call(
        middle_kernel,
        name="middle",
        compiler_params=pltpu.CompilerParams(vmem_limit_bytes=24 * 2**20),
        out_shape=shape((sections, kh, 128), BF16),
        in_specs=vmem(2),
        out_specs=HBM,
        scratch_shapes=[
            VMEM((blocks * vecs, sections * CAP), BF16),
            VMEM((128, sections * CAP), BF16),
            VMEM((kh, sections * CAP), BF16),
            VMEM((sections, kh, 128), BF16),
            pltpu.SemaphoreType.DMA((sections * CAP // 1024,)),
        ],
        cost_estimate=pl.CostEstimate(flops=10**9, bytes_accessed=2 * 10**6, transcendentals=0),
    )(received, mine)

    returned = lax.all_to_all(replies, AXES, split_axis=0, concat_axis=0, tiled=True)

    return pl.pallas_call(
        back_kernel,
        name="back",
        compiler_params=pltpu.CompilerParams(vmem_limit_bytes=53 * 2**20),
        out_shape=(shape((subs, vecs, inner), BF16), shape((subs, vecs, face), BF16)),
        in_specs=[SMEM] + vmem(3) + [HBM] * 3,
        out_specs=(HBM, HBM),
        scratch_shapes=[
            VMEM((subs, vecs, face), F32),
            VMEM((subs, inner, inner), BF16),
            VMEM((subs, face, inner), BF16),
            VMEM((16 * vecs, sections * CAP // 16), BF16),
            VMEM((subs, sections * CAP // 16, face), BF16),
            VMEM((subs, vecs, inner), BF16),
            VMEM((subs, vecs, face), BF16),
            pltpu.SemaphoreType.DMA((3,)),
            pltpu.SemaphoreType.DMA((subs + 1,)),
        ],
        cost_estimate=pl.CostEstimate(flops=3 * 10**9, bytes_accessed=6 * 10**6, transcendentals=0),
    )(live_count, returned, dest, interior_res, local, interior_inv, coupling)


def solution(mesh):
    rows = P(AXES)
    in_specs = (rows, rows, rows, rows, rows, P("grp"), rows, rows, rows)
    return jax.shard_map(
        on_device, mesh=mesh, in_specs=in_specs, out_specs=(rows, rows), check_vma=False
    )
```
